1024 devices in a mesh: comp: 4 (over y), ty: 8 (over z_lo), tx: 32 (over z_hi, x, core).
Axes of the slice: x: 4, y: 4, z: 32 (z_hi: 4, z_lo: 8; z = z_hi * 8 + z_lo), core: 2. Of those that a mesh axis runs over, the one named last changes fastest.
Arguments:
- ocean: float32 [3, 256, 8192], P(None, 'ty', 'tx'), may hold values from -4 to 4
- tracers: float32 [19, 8, 32, 8192], P(None, 'ty', 'comp', 'tx'), may hold values from 0.05 to 3
- bottom: int32 [256, 128], P('ty', 'tx'), may hold values from 0 to 64, as said below
- stoich: float32 [14], replicated, may hold values from -3 to 3
Outputs:
- ocean_out: float32 [3, 256, 8192], P(None, 'ty', 'tx')
- tracers_out: float32 [19, 8, 32, 8192], P(None, 'ty', 'comp', 'tx')
The draws below stay inside these ranges and needn't reach their ends.
Inputs may be any that keep to these rules, and one draw needn't show every extreme that they name: bottom counts wet levels from the surface; 0 marks land, 64 a full column.
All inputs are finite; a program needn't handle non-finite values.
Results may differ from the reference program's by a relative error of at most 0.0003.
Values sent between devices are 32-bit elements; how exact they have to be, the bound alone decides.
No kernel may reach another device: no remote copies, remote signals or barrier semaphores. Data moves between devices by JAX's collectives and lax.ppermute only.
A program may use at most 32 MiB of HBM per device.

```python
import math
import jax
import jax.numpy as jnp
from jax import lax

NTR = 19
LEV = 64
STEPS = 2
BANDS = 8
BAND = 32
NY = 256
NX = 128


def draw_bottom(key, part):
    raw_levels = jax.random.randint(key, (NY, NX), -16, LEV + 16)
    return jnp.clip(raw_levels, 0, LEV).astype(jnp.int32)


def steps_of(stream_key, dims, split, least, largest):
    loudness = 1.0
    for dim, parts in split:
        steps = jax.random.uniform(jax.random.fold_in(jax.random.fold_in(stream_key, 6), dim), (parts,), jnp.float32, least / len(split), largest / len(split))
        loudness = loudness * jnp.repeat(jnp.exp(steps), dims[dim] // parts).reshape((-1,) + (1,) * (len(dims) - 1 - dim))
    return loudness


def noise(rng, dims, deviation, bound, pieces=(), dtype=jnp.bfloat16):
    gain = steps_of(rng, dims, pieces, -0.22, 0.18) if pieces else 1.0
    entries = jax.random.normal(rng, dims, jnp.float32) * deviation * gain
    return jnp.minimum(jnp.maximum(entries, -bound), bound).astype(dtype)


def setup_inputs(seed: int = 0) -> dict:
    keys = jax.random.split(jax.random.key(seed), 5)
    return {
        "ocean": noise(keys[0], (3, NY, NX * LEV), 1.0, 4.0, ((1, 8), (2, 32)), jnp.float32),
        "tracers": jnp.clip(jnp.exp(math.log(3.0) - 4.0943445 * jax.random.uniform(keys[1], (NTR, BANDS, BAND, NX * LEV), jnp.float32) ** steps_of(keys[1], (NTR, BANDS, BAND, NX * LEV), ((1, 8), (2, 4), (3, 32)), -0.2, 0.2)), 0.05, 3.0),
        "bottom": draw_bottom(jax.random.fold_in(keys[4], 71), 0),
        "stoich": noise(keys[3], (NTR - 5,), 1.0, 3.0, (), jnp.float32),
    }


ATTEN_WATER = 0.04
ATTEN_CHL = 0.03
PRESSURE = 0.05
TIME_STEP = 0.2
CORIOLIS = 1.0
DAMPING = 0.05
HEAT_GAIN = 2.0
DIFFUSE = 0.2
ADVECT = 0.08
GROWTH = 1.0
HALF_LIGHT = 0.2
HALF_NUTRIENT = 0.5
TEMP_COEF = 0.1
GRAZE = 0.8
HALF_PREY = 0.3
MORTAL = 0.1
REMIN = 0.2
CHL_RELAX = 0.3
CHL_RATIO = 0.5
CHL_GAIN = 0.2
ASSIM = 0.3
GRAZER_LOSS = 0.05
REACT_STEP = 0.2


def level_sums(values, inclusive):
    count = values.shape[-1]
    level_ids = jnp.arange(count)
    if inclusive:
        ladder = level_ids[:, None] <= level_ids[None, :]
    else:
        ladder = level_ids[:, None] < level_ids[None, :]
    return jnp.dot(values, ladder.astype(jnp.float32), precision=lax.Precision.HIGHEST)


def optics(chloro, wet_mask):
    absorb = (ATTEN_WATER + ATTEN_CHL * jnp.maximum(chloro, 0.0)) * wet_mask
    sunlight = jnp.exp(-level_sums(absorb, False))
    heating = sunlight * (1.0 - jnp.exp(-absorb)) * wet_mask
    return sunlight, heating


def ocean_update(current, row_margin, column_margin, heating, wet_mask):
    east = current[0]
    north = current[1]
    temper = current[2]
    press_rows = PRESSURE * level_sums(row_margin, True)
    press_cols = PRESSURE * level_sums(column_margin, True)
    slope_x = 0.5 * (press_cols[:, 2:] - press_cols[:, :-2])
    slope_y = 0.5 * (press_rows[2:] - press_rows[:-2])
    spread = row_margin[2:] + row_margin[:-2] + column_margin[:, 2:] + column_margin[:, :-2] - 4.0 * temper
    new_east = wet_mask * ((1.0 - DAMPING) * east + TIME_STEP * (CORIOLIS * north - slope_x))
    new_north = wet_mask * ((1.0 - DAMPING) * north - TIME_STEP * (CORIOLIS * east + slope_y))
    new_temp = wet_mask * (temper + TIME_STEP * (HEAT_GAIN * heating + DIFFUSE * spread))
    return jnp.stack([new_east, new_north, new_temp])


def minmod(first, second):
    return jnp.where(first * second > 0.0, jnp.sign(first) * jnp.minimum(jnp.abs(first), jnp.abs(second)), 0.0)


def face_transport(field_wide, speed_wide, wet_wide, along_dim, cell_count):
    def window(values, offset):
        return lax.slice_in_dim(values, offset, offset + cell_count + 1, axis=along_dim)

    far_left = window(field_wide, 0)
    left_cell = window(field_wide, 1)
    right_cell = window(field_wide, 2)
    far_right = window(field_wide, 3)
    speed = 0.5 * (window(speed_wide, 1) + window(speed_wide, 2)) * window(wet_wide, 1) * window(wet_wide, 2)
    from_left = left_cell + 0.5 * minmod(left_cell - far_left, right_cell - left_cell)
    from_right = right_cell - 0.5 * minmod(right_cell - left_cell, far_right - right_cell)
    flux = ADVECT * speed * jnp.where(speed > 0.0, from_left, from_right)
    return lax.slice_in_dim(flux, 1, cell_count + 1, axis=along_dim) - lax.slice_in_dim(flux, 0, cell_count, axis=along_dim)


def reactions(advected, sunlight, temper, stoich, wet_mask):
    nutrient = jnp.maximum(advected[0], 0.0)
    phyto = jnp.maximum(advected[1], 0.0)
    chloro = jnp.maximum(advected[2], 0.0)
    grazer = jnp.maximum(advected[3], 0.0)
    detritus = jnp.maximum(advected[4], 0.0)
    uptake = GROWTH * sunlight / (sunlight + HALF_LIGHT) * nutrient / (nutrient + HALF_NUTRIENT) * jnp.exp(TEMP_COEF * temper)
    growth = uptake * phyto
    grazing = GRAZE * grazer * phyto * phyto / (phyto * phyto + HALF_PREY)
    dying = MORTAL * phyto
    remineral = REMIN * detritus
    core = jnp.stack([
        remineral - growth,
        growth - grazing - dying,
        CHL_RELAX * (CHL_RATIO * phyto - chloro) + CHL_GAIN * growth,
        ASSIM * grazing - GRAZER_LOSS * grazer,
        dying + (1.0 - ASSIM) * grazing + GRAZER_LOSS * grazer - remineral,
    ])
    others = stoich.reshape((stoich.shape[0],) + (1,) * growth.ndim) * (growth - remineral)[None]
    change_all = jnp.concatenate([core, others], axis=0)
    return (advected + REACT_STEP * change_all) * wet_mask[None]


def reference(ocean, tracers, bottom, stoich):
    current = ocean.reshape(3, NY, NX, LEV)
    tracer_now = tracers.reshape(NTR, NY, NX, LEV)
    wet_mask = (jnp.arange(LEV)[None, None, :] < bottom[:, :, None]).astype(jnp.float32)
    wet_cols = jnp.pad(wet_mask, ((0, 0), (2, 2), (0, 0)))
    wet_rows = jnp.pad(wet_mask, ((2, 2), (0, 0), (0, 0)))
    for step_index in range(STEPS):
        sunlight, heating = optics(tracer_now[2], wet_mask)
        temper = current[2]
        row_margin = jnp.pad(temper, ((1, 1), (0, 0), (0, 0)))
        column_margin = jnp.pad(temper, ((0, 0), (1, 1), (0, 0)))
        current = ocean_update(current, row_margin, column_margin, heating, wet_mask)
        east_wide = jnp.pad(current[0], ((0, 0), (2, 2), (0, 0)))
        north_wide = jnp.pad(current[1], ((2, 2), (0, 0), (0, 0)))

        def advect_one(tracer_field):
            column_change = face_transport(jnp.pad(tracer_field, ((0, 0), (2, 2), (0, 0))), east_wide, wet_cols, 1, NX)
            row_change = face_transport(jnp.pad(tracer_field, ((2, 2), (0, 0), (0, 0))), north_wide, wet_rows, 0, NY)
            return tracer_field - column_change - row_change

        advected = lax.map(advect_one, tracer_now)
        tracer_now = reactions(advected, sunlight, current[2], stoich, wet_mask)
    return current.reshape(ocean.shape), tracer_now.reshape(tracers.shape)
```

```python
import jax
import jax.numpy as jnp
from jax import lax
from jax.experimental import pallas as pl
from jax.experimental.pallas import tpu as pltpu
from jax.sharding import PartitionSpec as P

LEV = 64
NTR = 19
ROWS = 8
WIDE = 256
FIELDS = 22
U, V, T, WET = 19, 20, 21, 22
VMEM = pltpu.VMEM


def next_col(x):
    return pltpu.roll(x, x.shape[1] - LEV, 1)


def prev_col(x):
    return pltpu.roll(x, LEV, 1)


def next_row(x):
    return pltpu.roll(x, x.shape[0] - 1, 0)


def prev_row(x):
    return pltpu.roll(x, 1, 0)


def divergence(q, fac, nxt, prv):
    d = nxt(q) - q
    b = prv(d)
    m = jnp.where(d * b > 0.0, jnp.where(jnp.abs(d) < jnp.abs(b), d, b), 0.0)
    half = 0.5 * m
    flux = fac * jnp.where(fac > 0.0, q + half, nxt(q - half))
    return flux - prv(flux)


def face_factor(vel, wet, nxt):
    return 0.08 * (0.5 * (vel + nxt(vel)) * wet * nxt(wet))


def level_sum(x, ladder):
    rows, lanes = x.shape
    count = lanes // 128
    parts = [x[:, 128 * i : 128 * (i + 1)] for i in range(count)]
    out = jnp.dot(
        jnp.concatenate(parts, axis=0),
        ladder,
        precision=lax.Precision.HIGHEST,
        preferred_element_type=jnp.float32,
    )
    return jnp.concatenate([out[rows * i : rows * (i + 1)] for i in range(count)], axis=1)


def ladders():
    r = lax.broadcasted_iota(jnp.int32, (128, 128), 0)
    c = lax.broadcasted_iota(jnp.int32, (128, 128), 1)
    same = (r // LEV) == (c // LEV)
    incl = jnp.where(same & (r <= c), 1.0, 0.0).astype(jnp.float32)
    excl = jnp.where(same & (r < c), 1.0, 0.0).astype(jnp.float32)
    return incl, excl


def optics(chloro, wet, excl):
    absorb = (0.04 + 0.03 * jnp.maximum(chloro, 0.0)) * wet
    sun = jnp.exp(-level_sum(absorb, excl))
    heat = sun * (1.0 - jnp.exp(-absorb)) * wet
    return sun, heat


def reaction_terms(adv, sun, temp):
    n, p, c, z, d = [jnp.maximum(a, 0.0) for a in adv]
    uptake = sun / (sun + 0.2) * n / (n + 0.5) * jnp.exp(0.1 * temp)
    growth = uptake * p
    grazing = 0.8 * z * p * p / (p * p + 0.3)
    dying = 0.1 * p
    remin = 0.2 * d
    core = [
        remin - growth,
        growth - grazing - dying,
        0.3 * (0.5 * p - c) + 0.2 * growth,
        0.3 * grazing - 0.05 * z,
        dying + 0.7 * grazing + 0.05 * z - remin,
    ]
    return core, growth - remin


def odd(name):
    return lax.rem(lax.axis_index(name), 2) == 1


def pack_kernel(ocean_ref, tr_ref, bot_ref, out_ref):
    rows = pl.ds(pl.multiple_of(lax.axis_index("comp") * ROWS, ROWS), ROWS)
    for f in range(FIELDS):
        x = tr_ref[f, 0] if f < NTR else ocean_ref[f - NTR, rows, :]
        out_ref[2 * f] = x[:, :128]
        out_ref[2 * f + 1] = x[:, 128:]
    out_ref[2 * FIELDS] = jnp.zeros((ROWS, 128), jnp.float32)
    out_ref[2 * FIELDS, :, 0:4] = bot_ref[rows, :].astype(jnp.float32)


def wet_tiles(bottom):
    lane = lax.broadcasted_iota(jnp.int32, (ROWS, 128), 1)
    level = lax.rem(lane, LEV).astype(jnp.float32)
    tiles = []
    for h in range(2):
        b = jnp.where(lane < LEV, bottom[:, 2 * h : 2 * h + 1], bottom[:, 2 * h + 1 : 2 * h + 2])
        tiles.append(jnp.where(level < b, 1.0, 0.0))
    return tiles


def mid_kernel(own_ref, eo_ref, ee_ref, ext_ref, ne_ref, no_ref):
    flip = odd("tx")
    sub = lax.broadcasted_iota(jnp.int32, (ROWS, 128), 0)
    up = (sub < 4) == odd("comp")

    def west(t):
        return jnp.where(flip, ee_ref[t], eo_ref[t])

    def east(t):
        return jnp.where(flip, eo_ref[t], ee_ref[t])

    def put(f, blocks):
        for i, b in enumerate(blocks):
            ext_ref[f, :, 128 * i : 128 * (i + 1)] = b
        for k, (a, b) in enumerate(((blocks[2], blocks[3]), (blocks[1], blocks[4]))):
            swapped = pltpu.roll(b, 4, 0)
            ne_ref[2 * f + k] = jnp.where(up, a, swapped)
            no_ref[2 * f + k] = jnp.where(up, swapped, a)

    for f in range(FIELDS):
        a, b = 2 * f, 2 * f + 1
        put(f, [west(a), west(b), own_ref[a], own_ref[b], east(a), east(b)])
    t = 2 * FIELDS
    put(WET, wet_tiles(west(t)) + wet_tiles(own_ref[t]) + wet_tiles(east(t)))


def main_kernel(ext_ref, te_ref, to_ref, stoich_ref, ocean_ref, out_ref, h_ref, q_ref):
    incl, excl = ladders()
    sub = lax.broadcasted_iota(jnp.int32, (ROWS, 128), 0)
    first = (sub < 4) != odd("comp")

    def fill(f, _):
        for k, (ia, ib) in enumerate(((1, 2), (0, 3))):
            te, to = te_ref[2 * f + k], to_ref[2 * f + k]
            h_ref[f, :, 128 * ia : 128 * (ia + 1)] = jnp.where(first, te, to)
            h_ref[f, :, 128 * ib : 128 * (ib + 1)] = jnp.where(
                first, pltpu.roll(te, 4, 0), pltpu.roll(to, 4, 0)
            )
        return 0

    lax.fori_loop(0, FIELDS + 1, fill, 0)

    def both(o, h):
        return jnp.concatenate([o[:, 128:640], h], axis=0)

    u_o, v_o, t_o, w_o = [ext_ref[f] for f in (U, V, T, WET)]
    u_h, v_h, t_h, w_h = [h_ref[f] for f in (U, V, T, WET)]
    v_b, t_b, w_b = both(v_o, v_h), both(t_o, t_h), both(w_o, w_h)
    u_b = both(u_o, u_h)

    p_o = 0.05 * level_sum(t_o, incl)
    p_h = 0.05 * level_sum(t_h, incl)
    p_b = both(p_o, p_h)
    sun, heat = optics(both(ext_ref[2], h_ref[2]), w_b, excl)

    def east_speed(u, v, p, w):
        slope = 0.5 * (next_col(p) - prev_col(p))
        return w * (0.95 * u + 0.2 * (v - slope))

    def north_speed(u, v, p, w):
        slope = 0.5 * (next_row(p) - prev_row(p))
        return w * (0.95 * v - 0.2 * (u + slope))

    u1_o = east_speed(u_o, v_o, p_o, w_o)
    u1_h = east_speed(u_h, v_h, p_h, w_h)
    v1_b = north_speed(u_b, v_b, p_b, w_b)
    spread = (
        next_row(t_b)
        + prev_row(t_b)
        + both(next_col(t_o), next_col(t_h))
        + both(prev_col(t_o), prev_col(t_h))
        - 4.0 * t_b
    )
    t1_b = w_b * (t_b + 0.2 * (2.0 * heat + 0.2 * spread))

    fc_o = face_factor(u1_o, w_o, next_col)
    fc_h = face_factor(u1_h, w_h, next_col)
    fr_b = face_factor(v1_b, w_b, next_row)

    def advect1(f):
        q_o, q_h = ext_ref[f], h_ref[f]
        q_b = both(q_o, q_h)
        col = both(
            divergence(q_o, fc_o, next_col, prev_col), divergence(q_h, fc_h, next_col, prev_col)
        )
        return q_b - col - divergence(q_b, fr_b, next_row, prev_row)

    def keep1(f, _):
        q_ref[f] = advect1(f)
        return 0

    lax.fori_loop(0, 5, keep1, 0)
    core, gain = reaction_terms([q_ref[f] for f in range(5)], sun, t1_b)
    for f in range(5):
        q_ref[f] = (q_ref[f] + 0.2 * core[f]) * w_b

    def others1(f, _):
        q_ref[f] = (advect1(f) + 0.2 * (stoich_ref[f - 5] * gain)) * w_b
        return 0

    lax.fori_loop(5, NTR, others1, 0)

    own = slice(128, 384)
    w2 = w_b[:ROWS]
    w_own = w2[:, own]
    u1 = both(u1_o, u1_h)
    p1 = 0.05 * level_sum(t1_b, incl)
    sun2, heat2 = optics(q_ref[2, :ROWS, own], w_own, excl)
    u2 = east_speed(u1[:ROWS], v1_b[:ROWS], p1[:ROWS], w2)
    v2 = north_speed(u1[:, own], v1_b[:, own], p1[:, own], w_b[:, own])
    t1 = t1_b[:ROWS, own]
    spread2 = (
        next_row(t1_b)[:ROWS, own]
        + prev_row(t1_b)[:ROWS, own]
        + next_col(t1_b[:ROWS])[:, own]
        + prev_col(t1_b[:ROWS])[:, own]
        - 4.0 * t1
    )
    t2 = w_own * (t1 + 0.2 * (2.0 * heat2 + 0.2 * spread2))
    for peer in range(4):
        ocean_ref[peer, 0] = u2[:, own]
        ocean_ref[peer, 1] = v2[:ROWS]
        ocean_ref[peer, 2] = t2

    fc2 = face_factor(u2, w2, next_col)
    fr2 = face_factor(v2, w_b[:, own], next_row)

    def advect2(f):
        col = divergence(q_ref[f, :ROWS], fc2, next_col, prev_col)[:, own]
        row = divergence(q_ref[f, :, own], fr2, next_row, prev_row)[:ROWS]
        return q_ref[f, :ROWS, own] - col - row

    adv = [advect2(f) for f in range(5)]
    core2, gain2 = reaction_terms(adv, sun2, t2)
    for f in range(5):
        out_ref[f, 0] = (adv[f] + 0.2 * core2[f]) * w_own

    def others2(f, _):
        out_ref[f, 0] = (advect2(f) + 0.2 * (stoich_ref[f - 5] * gain2)) * w_own
        return 0

    lax.fori_loop(5, NTR, others2, 0)


def swaps(count, first, place=lambda i: i):
    pairs = []
    for a in range(first, count - 1, 2):
        pairs += [(place(a), place(a + 1)), (place(a + 1), place(a))]
    return pairs


def shards(ocean, tracers, bottom, stoich):
    comps = lax.axis_size("comp")
    bands = lax.axis_size("ty")
    tiles = lax.axis_size("tx")
    vmem = pl.BlockSpec(memory_space=VMEM)

    def arr(*dims):
        return jax.ShapeDtypeStruct(dims, jnp.float32)

    def place(row):
        return (row % comps) * bands + row // comps

    packed = pl.pallas_call(
        pack_kernel,
        out_shape=arr(2 * FIELDS + 1, ROWS, 128),
        in_specs=[vmem] * 3,
        out_specs=vmem,
    )(ocean, tracers, bottom)
    from_odd = lax.ppermute(packed, "tx", swaps(tiles, 1))
    from_even = lax.ppermute(packed, "tx", swaps(tiles, 0))
    ext, ne, no = pl.pallas_call(
        mid_kernel,
        out_shape=(
            arr(FIELDS + 1, ROWS, 768),
            arr(2 * FIELDS + 2, ROWS, 128),
            arr(2 * FIELDS + 2, ROWS, 128),
        ),
        in_specs=[vmem] * 3,
        out_specs=(vmem,) * 3,
    )(packed, from_odd, from_even)
    axes = ("comp", "ty")
    te = lax.ppermute(ne, axes, swaps(comps * bands, 0, place))
    to = lax.ppermute(no, axes, swaps(comps * bands, 1, place))
    rows, tracers_out = pl.pallas_call(
        main_kernel,
        out_shape=(arr(comps, 3, ROWS, WIDE), arr(NTR, 1, ROWS, WIDE)),
        in_specs=[vmem] * 3 + [pl.BlockSpec(memory_space=pltpu.SMEM)],
        out_specs=(vmem, vmem),
        scratch_shapes=[
            VMEM((FIELDS + 1, ROWS, 512), jnp.float32),
            VMEM((NTR, 2 * ROWS, 512), jnp.float32),
        ],
    )(ext, te, to, stoich)
    gathered = lax.all_to_all(rows, "comp", 0, 0, tiled=True)
    ocean_out = jnp.swapaxes(gathered, 0, 1).reshape(3, comps * ROWS, WIDE)
    return ocean_out, tracers_out


def solution(mesh):
    in_specs = (P(None, "ty", "tx"), P(None, "ty", "comp", "tx"), P("ty", "tx"), P())
    out_specs = (P(None, "ty", "tx"), P(None, "ty", "comp", "tx"))
    return jax.shard_map(shards, mesh=mesh, in_specs=in_specs, out_specs=out_specs, check_vma=False)
```

```python
import jax
import jax.numpy as jnp
from jax import lax
from jax.experimental import pallas as pl
from jax.experimental.pallas import tpu as pltpu
from jax.sharding import PartitionSpec as P


LEV = 64
NTR = 19
ROWS = 8
FIELDS = 22
U, V, T, WET = 19, 20, 21, 22
VMEM = pltpu.VMEM
TILE = (ROWS, 128)


def lanes():
    return lax.broadcasted_iota(jnp.int32, TILE, 1)


def subs():
    return lax.broadcasted_iota(jnp.int32, TILE, 0)


def half_turn(x):
    return pltpu.roll(x, LEV, 1)


def mix(a, b):
    return jnp.where(lanes() < LEV, a, b)


def narrow(x):
    return [mix(x[i + 2], x[i]) for i in range(len(x) - 2)]


def each(f, *lists):
    return [f(*args) for args in zip(*lists)]


def next_col(x):
    return x[1:] + [half_turn(x[0])]


def prev_col(x):
    return [half_turn(x[-1])] + x[:-1]


def next_row(o, h):
    edge = subs() == 0
    return (
        [pltpu.roll(jnp.where(edge, b, a), ROWS - 1, 0) for a, b in zip(o, h)],
        [pltpu.roll(jnp.where(edge, a, b), ROWS - 1, 0) for a, b in zip(o, h)],
    )


def prev_row(o, h):
    edge = subs() == ROWS - 1
    return (
        [pltpu.roll(jnp.where(edge, b, a), 1, 0) for a, b in zip(o, h)],
        [pltpu.roll(jnp.where(edge, a, b), 1, 0) for a, b in zip(o, h)],
    )


def minmod(a, b):
    return jnp.maximum(jnp.minimum(a, b), 0.0) + jnp.minimum(jnp.maximum(a, b), 0.0)


def upwind(fac, left, right):
    return fac * jnp.where(fac > 0.0, left, right)


def minus(x, y):
    return each(lambda a, b: a - b, x, y)


def col_divergence(q, fac):
    d = minus(next_col(q), q)
    m = each(minmod, d, prev_col(d))
    left = each(lambda a, b: (a + a) + b, q, m)
    right = each(lambda a, b: (a + a) - b, q, m)
    flux = each(upwind, fac, left, next_col(right))
    return minus(flux, prev_col(flux))


def row_divergence(o, h, fac_o, fac_h):
    n_o, n_h = next_row(o, h)
    d_o, d_h = minus(n_o, o), minus(n_h, h)
    b_o, b_h = prev_row(d_o, d_h)
    m_o, m_h = each(minmod, d_o, b_o), each(minmod, d_h, b_h)
    r_o = each(lambda a, b: (a + a) - b, o, m_o)
    r_h = each(lambda a, b: (a + a) - b, h, m_h)
    n_o, n_h = next_row(r_o, r_h)
    f_o = each(lambda f, a, b, c: upwind(f, (a + a) + b, c), fac_o, o, m_o, n_o)
    f_h = each(lambda f, a, b, c: upwind(f, (a + a) + b, c), fac_h, h, m_h, n_h)
    p_o, p_h = prev_row(f_o, f_h)
    return minus(f_o, p_o), minus(f_h, p_h)


def half_factor(vel, wet, next_vel, next_wet):
    return 0.5 * (0.08 * (0.5 * (vel + next_vel) * wet * next_wet))


def col_factor(vel, wet):
    return each(half_factor, vel, wet, next_col(vel), next_col(wet))


def row_factor(vel_o, vel_h, wet_o, wet_h):
    n_o, n_h = next_row(vel_o, vel_h)
    w_o, w_h = next_row(wet_o, wet_h)
    return each(half_factor, vel_o, wet_o, n_o, w_o), each(half_factor, vel_h, wet_h, n_h, w_h)


def level_sum(tiles, inclusive):
    r = lax.rem(lax.broadcasted_iota(jnp.int32, (256, 128), 0), 128)
    c = lax.broadcasted_iota(jnp.int32, (256, 128), 1)
    above = (r <= c) if inclusive else (r < c)
    ladder = jnp.where(((r < LEV) == (c < LEV)) & above, 1.0, 0.0).astype(jnp.bfloat16)
    x = jnp.concatenate(tiles, axis=0)
    major = x.astype(jnp.bfloat16)
    minor = (x - major.astype(jnp.float32)).astype(jnp.bfloat16)
    out = jnp.dot(
        jnp.concatenate([major, minor], axis=1), ladder, preferred_element_type=jnp.float32
    )
    return [out[ROWS * i : ROWS * (i + 1)] for i in range(len(tiles))]


def optics(chloro, wet):
    absorb = each(lambda a, w: (0.04 + 0.03 * jnp.maximum(a, 0.0)) * w, chloro, wet)
    sun = [jnp.exp(-s) for s in level_sum(absorb, False)]
    heat = each(lambda s, a, w: s * (1.0 - jnp.exp(-a)) * w, sun, absorb, wet)
    return sun, heat


def east_speed(u, v, p, w):
    return each(
        lambda u, v, e, b, w: w * (0.95 * u + 0.2 * (v - 0.5 * (e - b))),
        u, v, next_col(p), prev_col(p), w,
    )


def north_speed(u, v, n, b, w):
    return each(
        lambda u, v, n, b, w: w * (0.95 * v - 0.2 * (u + 0.5 * (n - b))), u, v, n, b, w
    )


def warmed(t, heat, n, s, e, b, w):
    return each(
        lambda t, heat, n, s, e, b, w: w
        * (t + 0.2 * (2.0 * heat + 0.2 * (n + s + e + b - 4.0 * t))),
        t, heat, n, s, e, b, w,
    )


def reaction(adv, sun, temp):
    n, p, c, z, d = [jnp.maximum(a, 0.0) for a in adv]
    uptake = sun / (sun + 0.2) * n / (n + 0.5) * jnp.exp(0.1 * temp)
    growth = uptake * p
    grazing = 0.8 * z * p * p / (p * p + 0.3)
    dying = 0.1 * p
    remin = 0.2 * d
    core = [
        remin - growth,
        growth - grazing - dying,
        0.3 * (0.5 * p - c) + 0.2 * growth,
        0.3 * grazing - 0.05 * z,
        dying + 0.7 * grazing + 0.05 * z - remin,
    ]
    return core, 0.2 * (growth - remin)


def odd(name):
    return lax.rem(lax.axis_index(name), 2) == 1


def pack_kernel(ocean_ref, tr_ref, bot_ref, out_ref):
    start = pl.multiple_of(lax.axis_index("comp") * ROWS, ROWS)
    rows = pl.ds(start, ROWS)
    for f in range(FIELDS):
        x = tr_ref[f, 0] if f < NTR else ocean_ref[f - NTR, rows, :]
        out_ref[2 * f] = x[:, :128]
        out_ref[2 * f + 1] = x[:, 128:]
    band = bot_ref.shape[1]
    row = lax.broadcasted_iota(jnp.int32, (ROWS, band), 0) + start
    pick = row == lax.broadcasted_iota(jnp.int32, (ROWS, band), 1)
    depth = jnp.zeros(TILE, jnp.float32)
    for c in range(4):
        line = bot_ref[c : c + 1, :].astype(jnp.float32)
        depth = jnp.where(
            lanes() == c, jnp.sum(jnp.where(pick, line, 0.0), axis=1, keepdims=True), depth
        )
    out_ref[2 * FIELDS] = depth


def wet_tiles(depth):
    level = lax.rem(lanes(), LEV).astype(jnp.float32)
    return [
        jnp.where(level < mix(depth[:, c : c + 1], depth[:, c + 1 : c + 2]), 1.0, 0.0)
        for c in (0, 2)
    ]


def mid_kernel(own_ref, eo_ref, ee_ref, ext_ref, ne_ref, no_ref):
    flip = odd("tx")
    keep = (subs() < 4) == odd("comp")

    def put(f, west, own, east):
        wide = []
        for low, high in ((west[0], own[1]), (west[1], east[0]), (own[0], east[1])):
            wide += [mix(low, half_turn(high)), mix(half_turn(low), high)]
        for i in range(6):
            ext_ref[f, i] = wide[i]
        m = narrow(wide)
        for k in range(2):
            turned = pltpu.roll(m[2 * k + 1], 4, 0)
            ne_ref[f, k] = jnp.where(keep, m[2 * k], turned)
            no_ref[f, k] = jnp.where(keep, turned, m[2 * k])

    def sides(t):
        a, b = eo_ref[t], ee_ref[t]
        return jnp.where(flip, b, a), own_ref[t], jnp.where(flip, a, b)

    def one(f, _):
        put(f, *zip(sides(2 * f), sides(2 * f + 1)))
        return 0

    lax.fori_loop(0, FIELDS, one, 0, unroll=2)
    put(WET, *[wet_tiles(x) for x in sides(2 * FIELDS)])


def main_kernel(
    ext_ref, te_ref, to_ref, stoich_ref, ocean_ref, out_ref, q_ref, co_ref, ch_ref, ro_ref,
    rh_ref, g_ref, w_ref, c2_ref, r2_ref, g2_ref,
):
    first = (subs() < 4) != odd("comp")

    def wide(f):
        return [ext_ref[f, i] for i in range(6)]

    def halo(f):
        out = []
        for k in range(2):
            te, to = te_ref[f, k], to_ref[f, k]
            out.append(jnp.where(first, te, to))
            out.append(pltpu.roll(jnp.where(first, to, te), 4, 0))
        return out

    def save(ref, tiles):
        for i, x in enumerate(tiles):
            ref[i] = x

    def load(ref):
        return [ref[i] for i in range(ref.shape[0])]

    u_w, v_w, t_w, w_w = [wide(f) for f in (U, V, T, WET)]
    u_h, v_h, t_h, w_h = [halo(f) for f in (U, V, T, WET)]
    u_m, v_m, t_m, w_m = [narrow(x) for x in (u_w, v_w, t_w, w_w)]
    w_six = w_m + narrow(w_h)
    save(w_ref, w_six)

    press = [0.05 * s for s in level_sum(t_w + t_h, True)]
    p_w, p_h = press[:6], press[6:]
    sun, heat = optics(narrow(wide(2)) + narrow(halo(2)), w_six)

    u1_w = east_speed(u_w, v_w, p_w, w_w)
    u1_h = east_speed(u_h, v_h, p_h, w_h)
    u1_m = narrow(u1_w)
    p_m = narrow(p_w)
    (n_m, n_h), (b_m, b_h) = next_row(p_m, p_h), prev_row(p_m, p_h)
    v1_m = north_speed(u_m, v_m, n_m, b_m, w_m)
    v1_h = north_speed(u_h, v_h, n_h, b_h, w_h)
    (n_m, n_h), (b_m, b_h) = next_row(t_m, t_h), prev_row(t_m, t_h)
    t1 = warmed(
        t_m + narrow(t_h),
        heat,
        n_m + narrow(n_h),
        b_m + narrow(b_h),
        narrow(next_col(t_w)) + narrow(next_col(t_h)),
        narrow(prev_col(t_w)) + narrow(prev_col(t_h)),
        w_six,
    )

    save(co_ref, col_factor(u1_w, w_w))
    save(ch_ref, col_factor(u1_h, w_h))
    fr_o, fr_h = row_factor(v1_m, v1_h, w_m, w_h)
    save(ro_ref, fr_o)
    save(rh_ref, fr_h)

    def advect1(f):
        q_w, q_h = wide(f), halo(f)
        q_m = narrow(q_w)
        r_m, r_h = row_divergence(q_m, q_h, load(ro_ref), load(rh_ref))
        a_m = minus(minus(q_m, narrow(col_divergence(q_w, load(co_ref)))), r_m)
        a_h = minus(minus(q_h, col_divergence(q_h, load(ch_ref))), r_h)
        return a_m + narrow(a_h)

    core_fields = [advect1(f) for f in range(5)]
    gain = []
    for i in range(6):
        core, g = reaction([core_fields[f][i] for f in range(5)], sun[i], t1[i])
        gain.append(g)
        for f in range(5):
            q_ref[f, i] = (core_fields[f][i] + 0.2 * core[f]) * w_six[i]
    save(g_ref, gain)

    def others1(f, _):
        s = stoich_ref[f - 5]
        out = each(lambda a, g, w: (a + s * g) * w, advect1(f), load(g_ref), load(w_ref))
        for i in range(6):
            q_ref[f, i] = out[i]
        return 0

    lax.fori_loop(5, NTR, others1, 0, unroll=2)

    t1_m, t1_o, t1_h = t1[:4], narrow(t1[:4]), t1[4:]
    w_o, w_oh = narrow(w_m), w_six[4:]
    p1 = [0.05 * s for s in level_sum(t1, True)]
    u2_m = east_speed(u1_m, v1_m, p1[:4], w_m)
    (n_o, n_h), (b_o, b_h) = next_row(narrow(p1[:4]), p1[4:]), prev_row(narrow(p1[:4]), p1[4:])
    v2_o = north_speed(narrow(u1_m), narrow(v1_m), n_o, b_o, w_o)
    v2_h = north_speed(narrow(u1_h), narrow(v1_h), n_h, b_h, w_oh)
    sun2, heat2 = optics(narrow([q_ref[2, i] for i in range(4)]), w_o)
    t2 = warmed(
        t1_o,
        heat2,
        next_row(t1_o, t1_h)[0],
        prev_row(t1_o, t1_h)[0],
        narrow(next_col(t1_m)),
        narrow(prev_col(t1_m)),
        w_o,
    )

    def plain(x):
        return [mix(x[0], half_turn(x[1])), mix(half_turn(x[0]), x[1])]

    for k, x in enumerate((narrow(u2_m), v2_o, t2)):
        for i, tile in enumerate(plain(x)):
            for peer in range(ocean_ref.shape[0]):
                ocean_ref[peer, k, :, 128 * i : 128 * (i + 1)] = tile

    save(c2_ref, col_factor(u2_m, w_m))
    fr_o, fr_h = row_factor(v2_o, v2_h, w_o, w_oh)
    save(r2_ref, fr_o + fr_h)

    def advect2(f):
        q_m = [q_ref[f, i] for i in range(4)]
        q_h = [q_ref[f, 4 + i] for i in range(2)]
        q_o = narrow(q_m)
        fr = load(r2_ref)
        row = row_divergence(q_o, q_h, fr[:2], fr[2:])[0]
        return minus(minus(q_o, narrow(col_divergence(q_m, load(c2_ref)))), row)

    def finish(f, tiles):
        for i, x in enumerate(plain(tiles)):
            out_ref[f, 0, :, 128 * i : 128 * (i + 1)] = x

    core_fields = [advect2(f) for f in range(5)]
    done = [[] for _ in range(5)]
    gain = []
    for i in range(2):
        core, g = reaction([core_fields[f][i] for f in range(5)], sun2[i], t2[i])
        gain.append(g)
        for f in range(5):
            done[f].append((core_fields[f][i] + 0.2 * core[f]) * w_o[i])
    for f in range(5):
        finish(f, done[f])
    save(g2_ref, gain + w_o)

    def others2(f, _):
        s = stoich_ref[f - 5]
        k = load(g2_ref)
        finish(f, each(lambda a, g, w: (a + s * g) * w, advect2(f), k[:2], k[2:]))
        return 0

    lax.fori_loop(5, NTR, others2, 0, unroll=2)


def swaps(count, first, place=lambda i: i):
    pairs = []
    for a in range(first, count - 1, 2):
        pairs += [(place(a), place(a + 1)), (place(a + 1), place(a))]
    return pairs


def shards(ocean, tracers, bottom, stoich):
    comps = lax.axis_size("comp")
    bands = lax.axis_size("ty")
    tiles = lax.axis_size("tx")
    vmem = pl.BlockSpec(memory_space=VMEM)

    def arr(*dims):
        return VMEM(dims, jnp.float32)

    def near(*args):
        return [pltpu.with_memory_space_constraint(a, VMEM) for a in args]

    def place(row):
        return (row % comps) * bands + row // comps

    packed = pl.pallas_call(
        pack_kernel,
        out_shape=arr(2 * FIELDS + 1, *TILE),
        in_specs=[vmem] * 3,
        out_specs=vmem,
    )(ocean, tracers, bottom.T)
    from_odd = lax.ppermute(packed, "tx", swaps(tiles, 1))
    from_even = lax.ppermute(packed, "tx", swaps(tiles, 0))
    ext, ne, no = pl.pallas_call(
        mid_kernel,
        out_shape=(
            arr(FIELDS + 1, 6, *TILE),
            arr(FIELDS + 1, 2, *TILE),
            arr(FIELDS + 1, 2, *TILE),
        ),
        in_specs=[vmem] * 3,
        out_specs=(vmem,) * 3,
    )(*near(packed, from_odd, from_even))
    axes = ("comp", "ty")
    te = lax.ppermute(ne, axes, swaps(comps * bands, 0, place))
    to = lax.ppermute(no, axes, swaps(comps * bands, 1, place))
    rows, tracers_out = pl.pallas_call(
        main_kernel,
        out_shape=(arr(comps, 3, ROWS, 256), jax.ShapeDtypeStruct((NTR, 1, ROWS, 256), jnp.float32)),
        in_specs=[vmem] * 3 + [pl.BlockSpec(memory_space=pltpu.SMEM)],
        out_specs=(vmem, vmem),
        scratch_shapes=[
            VMEM((n, *TILE) if isinstance(n, int) else (*n, *TILE), jnp.float32)
            for n in ((NTR, 6), 6, 4, 4, 4, 6, 6, 4, 4, 4)
        ],
    )(*near(ext, te, to), stoich)
    gathered = lax.all_to_all(rows, "comp", 0, 0, tiled=True)
    ocean_out = jnp.swapaxes(gathered, 0, 1).reshape(3, comps * ROWS, 256)
    return ocean_out, tracers_out


def solution(mesh):
    in_specs = (P(None, "ty", "tx"), P(None, "ty", "comp", "tx"), P("ty", "tx"), P())
    out_specs = (P(None, "ty", "tx"), P(None, "ty", "comp", "tx"))
    return jax.shard_map(shards, mesh=mesh, in_specs=in_specs, out_specs=out_specs, check_vma=False)
```

```python
import jax
import jax.numpy as jnp
from jax import lax
from jax.experimental import pallas as pl
from jax.experimental.pallas import tpu as pltpu
from jax.sharding import PartitionSpec as P


LEV = 64
NTR = 19
ROWS = 8
FIELDS = 22
U, V, T, WET = 19, 20, 21, 22
VMEM = pltpu.VMEM
TILE = (ROWS, 128)


def lanes():
    return lax.broadcasted_iota(jnp.int32, TILE, 1)


def subs():
    return lax.broadcasted_iota(jnp.int32, TILE, 0)


def half_turn(x):
    return pltpu.roll(x, LEV, 1)


def mix(a, b):
    return jnp.where(lanes() < LEV, a, b)


def narrow(x):
    return [mix(x[i + 2], x[i]) for i in range(len(x) - 2)]


def each(f, *lists):
    return [f(*args) for args in zip(*lists)]


def next_col(x):
    return x[1:] + [half_turn(x[0])]


def prev_col(x):
    return [half_turn(x[-1])] + x[:-1]


def next_row(o, h):
    edge = subs() == 0
    return (
        [pltpu.roll(jnp.where(edge, b, a), ROWS - 1, 0) for a, b in zip(o, h)],
        [pltpu.roll(jnp.where(edge, a, b), ROWS - 1, 0) for a, b in zip(o, h)],
    )


def prev_row(o, h):
    edge = subs() == ROWS - 1
    return (
        [pltpu.roll(jnp.where(edge, b, a), 1, 0) for a, b in zip(o, h)],
        [pltpu.roll(jnp.where(edge, a, b), 1, 0) for a, b in zip(o, h)],
    )


def minmod(a, b):
    return jnp.maximum(jnp.minimum(a, b), jnp.minimum(jnp.maximum(a, b), 0.0))


def upwind(fac, left, right):
    return fac * jnp.where(fac > 0.0, left, right)


def minus(x, y):
    return each(lambda a, b: a - b, x, y)


def col_divergence(q, fac):
    d = minus(next_col(q), q)
    m = each(minmod, d, prev_col(d))
    left = each(lambda a, b: (a + a) + b, q, m)
    right = each(lambda a, b: (a + a) - b, q, m)
    flux = each(upwind, fac, left, next_col(right))
    return minus(flux, prev_col(flux))


def row_divergence(o, h, fac_o, fac_h):
    n_o, n_h = next_row(o, h)
    d_o, d_h = minus(n_o, o), minus(n_h, h)
    b_o, b_h = prev_row(d_o, d_h)
    m_o, m_h = each(minmod, d_o, b_o), each(minmod, d_h, b_h)
    r_o = each(lambda a, b: (a + a) - b, o, m_o)
    r_h = each(lambda a, b: (a + a) - b, h, m_h)
    n_o, n_h = next_row(r_o, r_h)
    f_o = each(lambda f, a, b, c: upwind(f, (a + a) + b, c), fac_o, o, m_o, n_o)
    f_h = each(lambda f, a, b, c: upwind(f, (a + a) + b, c), fac_h, h, m_h, n_h)
    p_o, p_h = prev_row(f_o, f_h)
    return minus(f_o, p_o), minus(f_h, p_h)


def half_factor(vel, wet, next_vel, next_wet):
    return 0.5 * (0.08 * (0.5 * (vel + next_vel) * wet * next_wet))


def col_factor(vel, wet):
    return each(half_factor, vel, wet, next_col(vel), next_col(wet))


def row_factor(vel_o, vel_h, wet_o, wet_h):
    n_o, n_h = next_row(vel_o, vel_h)
    w_o, w_h = next_row(wet_o, wet_h)
    return each(half_factor, vel_o, wet_o, n_o, w_o), each(half_factor, vel_h, wet_h, n_h, w_h)


def level_sum(tiles, inclusive):
    r = lax.rem(lax.broadcasted_iota(jnp.int32, (256, 128), 0), 128)
    c = lax.broadcasted_iota(jnp.int32, (256, 128), 1)
    above = (r <= c) if inclusive else (r < c)
    ladder = jnp.where(((r < LEV) == (c < LEV)) & above, 1.0, 0.0).astype(jnp.bfloat16)
    x = jnp.concatenate(tiles, axis=0)
    major = x.astype(jnp.bfloat16)
    minor = (x - major.astype(jnp.float32)).astype(jnp.bfloat16)
    out = jnp.dot(
        jnp.concatenate([major, minor], axis=1), ladder, preferred_element_type=jnp.float32
    )
    return [out[ROWS * i : ROWS * (i + 1)] for i in range(len(tiles))]


def optics(chloro, wet):
    absorb = each(lambda a, w: (0.04 + 0.03 * jnp.maximum(a, 0.0)) * w, chloro, wet)
    sun = [jnp.exp(-s) for s in level_sum(absorb, False)]
    heat = each(lambda s, a, w: s * (1.0 - jnp.exp(-a)) * w, sun, absorb, wet)
    return sun, heat


def east_speed(u, v, p, w):
    return each(
        lambda u, v, e, b, w: w * (0.95 * u + 0.2 * (v - 0.5 * (e - b))),
        u, v, next_col(p), prev_col(p), w,
    )


def north_speed(u, v, n, b, w):
    return each(
        lambda u, v, n, b, w: w * (0.95 * v - 0.2 * (u + 0.5 * (n - b))), u, v, n, b, w
    )


def warmed(t, heat, n, s, e, b, w):
    return each(
        lambda t, heat, n, s, e, b, w: w
        * (t + 0.2 * (2.0 * heat + 0.2 * (n + s + e + b - 4.0 * t))),
        t, heat, n, s, e, b, w,
    )


def reaction(adv, sun, temp):
    n, p, c, z, d = [jnp.maximum(a, 0.0) for a in adv]
    uptake = sun / (sun + 0.2) * n / (n + 0.5) * jnp.exp(0.1 * temp)
    growth = uptake * p
    grazing = 0.8 * z * p * p / (p * p + 0.3)
    dying = 0.1 * p
    remin = 0.2 * d
    core = [
        remin - growth,
        growth - grazing - dying,
        0.3 * (0.5 * p - c) + 0.2 * growth,
        0.3 * grazing - 0.05 * z,
        dying + 0.7 * grazing + 0.05 * z - remin,
    ]
    return core, 0.2 * (growth - remin)


def odd(name):
    return lax.rem(lax.axis_index(name), 2) == 1


def wet_tiles(depth):
    level = lax.rem(lanes(), LEV).astype(jnp.float32)
    return [
        jnp.where(level < mix(depth[:, c : c + 1], depth[:, c + 1 : c + 2]), 1.0, 0.0)
        for c in (0, 2)
    ]


def strips(keep, a, b):
    turned = pltpu.roll(b, 4, 0)
    return jnp.where(keep, a, turned), jnp.where(keep, turned, a)


def unstrip(first, te, to):
    return jnp.where(first, te, to), pltpu.roll(jnp.where(first, to, te), 4, 0)


def pack_kernel(ocean_ref, tr_ref, bot_ref, out_ref, ne_ref, no_ref):
    start = pl.multiple_of(lax.axis_index("comp") * ROWS, ROWS)
    rows = pl.ds(start, ROWS)
    keep = (subs() < 4) == odd("comp")

    def strip(f, a, b):
        pair = strips(keep, mix(a, half_turn(b)), mix(half_turn(a), b))
        ne_ref[f], no_ref[f] = pair

    for f in range(FIELDS):
        x = tr_ref[f, 0] if f < NTR else ocean_ref[f - NTR, rows, :]
        a, b = x[:, :128], x[:, 128:]
        out_ref[2 * f] = a
        out_ref[2 * f + 1] = b
        strip(f, a, b)
    band = bot_ref.shape[1]
    row = lax.broadcasted_iota(jnp.int32, (ROWS, band), 0) + start
    pick = row == lax.broadcasted_iota(jnp.int32, (ROWS, band), 1)
    depth = jnp.zeros(TILE, jnp.float32)
    for c in range(4):
        line = bot_ref[c : c + 1, :].astype(jnp.float32)
        depth = jnp.where(
            lanes() == c, jnp.sum(jnp.where(pick, line, 0.0), axis=1, keepdims=True), depth
        )
    out_ref[2 * FIELDS] = depth
    strip(WET, *wet_tiles(depth))


def mid_kernel(own_ref, eo_ref, ee_ref, ext_ref, ne_ref, no_ref):
    flip = odd("tx")
    keep = (subs() < 4) == odd("comp")

    def put(f, west, own, east):
        wide = []
        for low, high in ((west[0], own[1]), (west[1], east[0]), (own[0], east[1])):
            wide += [mix(low, half_turn(high)), mix(half_turn(low), high)]
        for i in range(6):
            ext_ref[f, i] = wide[i]
        ne_ref[f], no_ref[f] = strips(keep, wide[2], wide[3])

    def sides(t):
        a, b = eo_ref[t], ee_ref[t]
        return jnp.where(flip, b, a), own_ref[t], jnp.where(flip, a, b)

    def one(f, _):
        put(f, *zip(sides(2 * f), sides(2 * f + 1)))
        return 0

    lax.fori_loop(0, FIELDS, one, 0, unroll=2)
    put(WET, *[wet_tiles(x) for x in sides(2 * FIELDS)])


def main_kernel(
    ext_ref, se_ref, so_ref, te_ref, to_ref, stoich_ref, ocean_ref, out_ref, q_ref, co_ref, ch_ref, ro_ref,
    rh_ref, g_ref, w_ref, c2_ref, r2_ref, g2_ref,
):
    first = (subs() < 4) != odd("comp")

    def wide(f):
        return [ext_ref[f, i] for i in range(6)]

    def halo(f):
        s0, s1 = unstrip(first, se_ref[f], so_ref[f])
        c0, c1 = unstrip(first, te_ref[f], to_ref[f])
        return [mix(c0, s0), mix(c1, s1), mix(s0, c0), mix(s1, c1)]

    def save(ref, tiles):
        for i, x in enumerate(tiles):
            ref[i] = x

    def load(ref):
        return [ref[i] for i in range(ref.shape[0])]

    u_w, v_w, t_w, w_w = [wide(f) for f in (U, V, T, WET)]
    u_h, v_h, t_h, w_h = [halo(f) for f in (U, V, T, WET)]
    u_m, v_m, t_m, w_m = [narrow(x) for x in (u_w, v_w, t_w, w_w)]
    w_six = w_m + narrow(w_h)
    save(w_ref, w_six)

    press = [0.05 * s for s in level_sum(t_w + t_h, True)]
    p_w, p_h = press[:6], press[6:]
    sun, heat = optics(narrow(wide(2)) + narrow(halo(2)), w_six)

    u1_w = east_speed(u_w, v_w, p_w, w_w)
    u1_h = east_speed(u_h, v_h, p_h, w_h)
    u1_m = narrow(u1_w)
    p_m = narrow(p_w)
    (n_m, n_h), (b_m, b_h) = next_row(p_m, p_h), prev_row(p_m, p_h)
    v1_m = north_speed(u_m, v_m, n_m, b_m, w_m)
    v1_h = north_speed(u_h, v_h, n_h, b_h, w_h)
    (n_m, n_h), (b_m, b_h) = next_row(t_m, t_h), prev_row(t_m, t_h)
    t1 = warmed(
        t_m + narrow(t_h),
        heat,
        n_m + narrow(n_h),
        b_m + narrow(b_h),
        narrow(next_col(t_w)) + narrow(next_col(t_h)),
        narrow(prev_col(t_w)) + narrow(prev_col(t_h)),
        w_six,
    )

    save(co_ref, col_factor(u1_w, w_w))
    save(ch_ref, col_factor(u1_h, w_h))
    fr_o, fr_h = row_factor(v1_m, v1_h, w_m, w_h)
    save(ro_ref, fr_o)
    save(rh_ref, fr_h)

    def advect1(f):
        q_w, q_h = wide(f), halo(f)
        q_m = narrow(q_w)
        r_m, r_h = row_divergence(q_m, q_h, load(ro_ref), load(rh_ref))
        a_m = minus(minus(q_m, narrow(col_divergence(q_w, load(co_ref)))), r_m)
        a_h = minus(minus(q_h, col_divergence(q_h, load(ch_ref))), r_h)
        return a_m + narrow(a_h)

    core_fields = [advect1(f) for f in range(5)]
    gain = []
    for i in range(6):
        core, g = reaction([core_fields[f][i] for f in range(5)], sun[i], t1[i])
        gain.append(g)
        for f in range(5):
            q_ref[f, i] = (core_fields[f][i] + 0.2 * core[f]) * w_six[i]
    save(g_ref, gain)

    def others1(f, _):
        s = stoich_ref[f - 5]
        out = each(lambda a, g, w: (a + s * g) * w, advect1(f), load(g_ref), load(w_ref))
        for i in range(6):
            q_ref[f, i] = out[i]
        return 0

    lax.fori_loop(5, NTR, others1, 0, unroll=2)

    t1_m, t1_o, t1_h = t1[:4], narrow(t1[:4]), t1[4:]
    w_o, w_oh = narrow(w_m), w_six[4:]
    p1 = [0.05 * s for s in level_sum(t1, True)]
    u2_m = east_speed(u1_m, v1_m, p1[:4], w_m)
    (n_o, n_h), (b_o, b_h) = next_row(narrow(p1[:4]), p1[4:]), prev_row(narrow(p1[:4]), p1[4:])
    v2_o = north_speed(narrow(u1_m), narrow(v1_m), n_o, b_o, w_o)
    v2_h = north_speed(narrow(u1_h), narrow(v1_h), n_h, b_h, w_oh)
    sun2, heat2 = optics(narrow([q_ref[2, i] for i in range(4)]), w_o)
    t2 = warmed(
        t1_o,
        heat2,
        next_row(t1_o, t1_h)[0],
        prev_row(t1_o, t1_h)[0],
        narrow(next_col(t1_m)),
        narrow(prev_col(t1_m)),
        w_o,
    )

    def plain(x):
        return [mix(x[0], half_turn(x[1])), mix(half_turn(x[0]), x[1])]

    for k, x in enumerate((narrow(u2_m), v2_o, t2)):
        for i, tile in enumerate(plain(x)):
            for peer in range(0, ocean_ref.shape[1], ROWS):
                ocean_ref[k, peer : peer + ROWS, 128 * i : 128 * (i + 1)] = tile

    save(c2_ref, col_factor(u2_m, w_m))
    fr_o, fr_h = row_factor(v2_o, v2_h, w_o, w_oh)
    save(r2_ref, fr_o + fr_h)

    def advect2(f):
        q_m = [q_ref[f, i] for i in range(4)]
        q_h = [q_ref[f, 4 + i] for i in range(2)]
        q_o = narrow(q_m)
        fr = load(r2_ref)
        row = row_divergence(q_o, q_h, fr[:2], fr[2:])[0]
        return minus(minus(q_o, narrow(col_divergence(q_m, load(c2_ref)))), row)

    def finish(f, tiles):
        for i, x in enumerate(plain(tiles)):
            out_ref[f, 0, :, 128 * i : 128 * (i + 1)] = x

    core_fields = [advect2(f) for f in range(5)]
    done = [[] for _ in range(5)]
    gain = []
    for i in range(2):
        core, g = reaction([core_fields[f][i] for f in range(5)], sun2[i], t2[i])
        gain.append(g)
        for f in range(5):
            done[f].append((core_fields[f][i] + 0.2 * core[f]) * w_o[i])
    for f in range(5):
        finish(f, done[f])
    save(g2_ref, gain + w_o)

    def others2(f, _):
        s = stoich_ref[f - 5]
        k = load(g2_ref)
        finish(f, each(lambda a, g, w: (a + s * g) * w, advect2(f), k[:2], k[2:]))
        return 0

    lax.fori_loop(5, NTR, others2, 0, unroll=2)


def swaps(count, first, place=lambda i: i):
    pairs = []
    for a in range(first, count - 1, 2):
        pairs += [(place(a), place(a + 1)), (place(a + 1), place(a))]
    return pairs


def shards(ocean, tracers, bottom, stoich):
    comps = lax.axis_size("comp")
    bands = lax.axis_size("ty")
    tiles = lax.axis_size("tx")
    vmem = pl.BlockSpec(memory_space=VMEM)

    def arr(*dims):
        return VMEM(dims, jnp.float32)

    def near(*args):
        return [pltpu.with_memory_space_constraint(a, VMEM) for a in args]

    def place(row):
        return (row % comps) * bands + row // comps

    packed, strip_e, strip_o = pl.pallas_call(
        pack_kernel,
        out_shape=(arr(2 * FIELDS + 1, *TILE), arr(FIELDS + 1, *TILE), arr(FIELDS + 1, *TILE)),
        in_specs=[vmem] * 3,
        out_specs=(vmem,) * 3,
    )(ocean, tracers, bottom.T)
    axes = ("comp", "ty")
    even_rows = swaps(comps * bands, 0, place)
    odd_rows = swaps(comps * bands, 1, place)
    from_odd = lax.ppermute(packed, "tx", swaps(tiles, 1))
    from_even = lax.ppermute(packed, "tx", swaps(tiles, 0))
    so = lax.ppermute(strip_o, axes, odd_rows)
    se = lax.ppermute(strip_e, axes, even_rows)
    ext, ne, no = pl.pallas_call(
        mid_kernel,
        out_shape=(arr(FIELDS + 1, 6, *TILE), arr(FIELDS + 1, *TILE), arr(FIELDS + 1, *TILE)),
        in_specs=[vmem] * 3,
        out_specs=(vmem,) * 3,
    )(*near(packed, from_odd, from_even))
    to = lax.ppermute(no, axes, odd_rows)
    te = lax.ppermute(ne, axes, even_rows)
    rows, tracers_out = pl.pallas_call(
        main_kernel,
        out_shape=(
            arr(3, comps * ROWS, 256),
            jax.ShapeDtypeStruct((NTR, 1, ROWS, 256), jnp.float32),
        ),
        in_specs=[vmem] * 5 + [pl.BlockSpec(memory_space=pltpu.SMEM)],
        out_specs=(vmem, vmem),
        scratch_shapes=[
            VMEM((n, *TILE) if isinstance(n, int) else (*n, *TILE), jnp.float32)
            for n in ((NTR, 6), 6, 4, 4, 4, 6, 6, 4, 4, 4)
        ],
    )(*near(ext, se, so, te, to), stoich)
    return lax.all_to_all(rows, "comp", 1, 1, tiled=True), tracers_out


def solution(mesh):
    in_specs = (P(None, "ty", "tx"), P(None, "ty", "comp", "tx"), P("ty", "tx"), P())
    out_specs = (P(None, "ty", "tx"), P(None, "ty", "comp", "tx"))
    return jax.shard_map(shards, mesh=mesh, in_specs=in_specs, out_specs=out_specs, check_vma=False)
```

```python
import jax
import jax.numpy as jnp
from jax import lax
from jax.experimental import pallas as pl
from jax.experimental.pallas import tpu as pltpu
from jax.sharding import PartitionSpec as P


LEV = 64
NTR = 19
ROWS = 8
FIELDS = 22
U, V, T, WET = 19, 20, 21, 22
PAIRS = 12
AUX = (
    "w_s", "p_e", "p_h", "sun_e", "sun_h", "heat_e", "heat_h", "cols_e", "rows_h", "u1_s",
    "u1_e", "v1_s", "v1_h", "t1_s", "sun2", "heat2",
)
VMEM = pltpu.VMEM
TILE = (ROWS, 128)


def lanes():
    return lax.broadcasted_iota(jnp.int32, TILE, 1)


def subs():
    return lax.broadcasted_iota(jnp.int32, TILE, 0)


def half_turn(x):
    return pltpu.roll(x, LEV, 1)


def mix(a, b):
    return jnp.where(lanes() < LEV, a, b)


def own_of(w):
    return [mix(w[4], w[0]), mix(w[5], w[1])]


def edge_of(w):
    return [w[2], w[3]]


def each(f, *lists):
    return [f(*args) for args in zip(*lists)]


def next_col(x):
    return x[1:] + [half_turn(x[0])]


def prev_col(x):
    return [half_turn(x[-1])] + x[:-1]


def next_split(s, e):
    return [s[1], mix(half_turn(s[0]), e[0])], [e[1], s[0]]


def prev_split(s, e):
    return [mix(e[1], half_turn(s[1])), s[0]], [s[1], e[0]]


def next_row(o, h):
    edge = subs() == 0
    return (
        [pltpu.roll(jnp.where(edge, b, a), ROWS - 1, 0) for a, b in zip(o, h)],
        [pltpu.roll(jnp.where(edge, a, b), ROWS - 1, 0) for a, b in zip(o, h)],
    )


def prev_row(o, h):
    edge = subs() == ROWS - 1
    return (
        [pltpu.roll(jnp.where(edge, b, a), 1, 0) for a, b in zip(o, h)],
        [pltpu.roll(jnp.where(edge, a, b), 1, 0) for a, b in zip(o, h)],
    )


def minmod(a, b):
    return jnp.maximum(jnp.minimum(a, b), jnp.minimum(jnp.maximum(a, b), 0.0))


def upwind(fac, left, right):
    return fac * jnp.where(fac > 0.0, left, right)


def minus(x, y):
    return each(lambda a, b: a - b, x, y)


def col_divergence(q, fac):
    d = minus(next_col(q), q)
    m = each(minmod, d, prev_col(d))
    left = each(lambda a, b: (a + a) + b, q, m)
    right = each(lambda a, b: (a + a) - b, q, m)
    flux = each(upwind, fac, left, next_col(right))
    return minus(flux, prev_col(flux))


def split_divergence(s, e, fac_s, fac_e):
    n_s, n_e = next_split(s, e)
    d_s, d_e = minus(n_s, s), minus(n_e, e)
    b_s, b_e = prev_split(d_s, d_e)
    m_s, m_e = each(minmod, d_s, b_s), each(minmod, d_e, b_e)
    r_s = each(lambda a, b: (a + a) - b, s, m_s)
    r_e = each(lambda a, b: (a + a) - b, e, m_e)
    n_s, n_e = next_split(r_s, r_e)
    f_s = each(lambda f, a, b, c: upwind(f, (a + a) + b, c), fac_s, s, m_s, n_s)
    f_e = each(lambda f, a, b, c: upwind(f, (a + a) + b, c), fac_e, e, m_e, n_e)
    return minus(f_s, prev_split(f_s, f_e)[0])


def row_divergence(o, h, fac_o, fac_h):
    n_o, n_h = next_row(o, h)
    d_o, d_h = minus(n_o, o), minus(n_h, h)
    b_o, b_h = prev_row(d_o, d_h)
    m_o, m_h = each(minmod, d_o, b_o), each(minmod, d_h, b_h)
    r_o = each(lambda a, b: (a + a) - b, o, m_o)
    r_h = each(lambda a, b: (a + a) - b, h, m_h)
    n_o, n_h = next_row(r_o, r_h)
    f_o = each(lambda f, a, b, c: upwind(f, (a + a) + b, c), fac_o, o, m_o, n_o)
    f_h = each(lambda f, a, b, c: upwind(f, (a + a) + b, c), fac_h, h, m_h, n_h)
    p_o, p_h = prev_row(f_o, f_h)
    return minus(f_o, p_o), minus(f_h, p_h)


def half_factor(vel, wet, next_vel, next_wet):
    return 0.5 * (0.08 * (0.5 * (vel + next_vel) * wet * next_wet))


def col_factor(vel, wet):
    return each(half_factor, vel, wet, next_col(vel), next_col(wet))


def split_factor(vel_s, vel_e, wet_s, wet_e):
    n_s, n_e = next_split(vel_s, vel_e)
    w_s, w_e = next_split(wet_s, wet_e)
    return each(half_factor, vel_s, wet_s, n_s, w_s), each(half_factor, vel_e, wet_e, n_e, w_e)


def row_factor(vel_o, vel_h, wet_o, wet_h):
    n_o, n_h = next_row(vel_o, vel_h)
    w_o, w_h = next_row(wet_o, wet_h)
    return each(half_factor, vel_o, wet_o, n_o, w_o), each(half_factor, vel_h, wet_h, n_h, w_h)


def level_sum(tiles, inclusive):
    r = lax.rem(lax.broadcasted_iota(jnp.int32, (256, 128), 0), 128)
    c = lax.broadcasted_iota(jnp.int32, (256, 128), 1)
    above = (r <= c) if inclusive else (r < c)
    ladder = jnp.where(((r < LEV) == (c < LEV)) & above, 1.0, 0.0).astype(jnp.bfloat16)
    x = jnp.concatenate(tiles, axis=0)
    major = x.astype(jnp.bfloat16)
    minor = (x - major.astype(jnp.float32)).astype(jnp.bfloat16)
    out = jnp.dot(
        jnp.concatenate([major, minor], axis=1), ladder, preferred_element_type=jnp.float32
    )
    return [out[ROWS * i : ROWS * (i + 1)] for i in range(len(tiles))]


def optics(chloro, wet):
    absorb = each(lambda a, w: (0.04 + 0.03 * jnp.maximum(a, 0.0)) * w, chloro, wet)
    sun = [jnp.exp(-s) for s in level_sum(absorb, False)]
    heat = each(lambda s, a, w: s * (1.0 - jnp.exp(-a)) * w, sun, absorb, wet)
    return sun, heat


def east_speed(u, v, n, b, w):
    return each(
        lambda u, v, n, b, w: w * (0.95 * u + 0.2 * (v - 0.5 * (n - b))), u, v, n, b, w
    )


def north_speed(u, v, n, b, w):
    return each(
        lambda u, v, n, b, w: w * (0.95 * v - 0.2 * (u + 0.5 * (n - b))), u, v, n, b, w
    )


def plus(x, y):
    return each(lambda a, b: a + b, x, y)


def warmed(t, heat, rows, cols, w):
    return each(
        lambda t, heat, r, c, w: w * (t + 0.2 * (2.0 * heat + 0.2 * (r + c - 4.0 * t))),
        t, heat, rows, cols, w,
    )


def reaction(adv, sun, temp):
    n, p, c, z, d = [jnp.maximum(a, 0.0) for a in adv]
    uptake = sun / (sun + 0.2) * n / (n + 0.5) * jnp.exp(0.1 * temp)
    growth = uptake * p
    grazing = 0.8 * z * p * p / (p * p + 0.3)
    dying = 0.1 * p
    remin = 0.2 * d
    core = [
        remin - growth,
        growth - grazing - dying,
        0.3 * (0.5 * p - c) + 0.2 * growth,
        0.3 * grazing - 0.05 * z,
        dying + 0.7 * grazing + 0.05 * z - remin,
    ]
    return core, 0.2 * (growth - remin)


def odd(name):
    return lax.rem(lax.axis_index(name), 2) == 1


def wet_tiles(depth):
    level = lax.rem(lanes(), LEV).astype(jnp.float32)
    return [
        jnp.where(level < mix(depth[:, c : c + 1], depth[:, c + 1 : c + 2]), 1.0, 0.0)
        for c in (0, 2)
    ]


def unstrip(below, above):
    first = subs() < 4
    return [
        jnp.where(first, below, above),
        pltpu.roll(jnp.where(first, above, below), 4, 0),
    ]


def pack_kernel(ocean_ref, tr_ref, bot_ref, stoich_ref, out_ref, up_ref, down_ref, yield_ref):
    for j in range(NTR - 5):
        yield_ref[j] = jnp.full(TILE, stoich_ref[j], jnp.float32)
    start = pl.multiple_of(lax.axis_index("comp") * ROWS, ROWS)
    rows = pl.ds(start, ROWS)

    def strip(f, a, b):
        a, b = mix(a, half_turn(b)), pltpu.roll(mix(half_turn(a), b), 4, 0)
        up_ref[f] = jnp.where(subs() < 4, a, b)
        down_ref[f] = jnp.where(subs() < 4, b, a)

    for f in range(FIELDS):
        x = tr_ref[f, 0] if f < NTR else ocean_ref[f - NTR, rows, :]
        a, b = x[:, :128], x[:, 128:]
        out_ref[2 * f] = a
        out_ref[2 * f + 1] = b
        strip(f, a, b)
    band = bot_ref.shape[1]
    row = lax.broadcasted_iota(jnp.int32, (ROWS, band), 0) + start
    pick = row == lax.broadcasted_iota(jnp.int32, (ROWS, band), 1)
    depth = jnp.zeros(TILE, jnp.float32)
    for c in range(4):
        line = bot_ref[c : c + 1, :].astype(jnp.float32)
        depth = jnp.where(
            lanes() == c, jnp.sum(jnp.where(pick, line, 0.0), axis=1, keepdims=True), depth
        )
    out_ref[2 * FIELDS] = depth
    strip(WET, *wet_tiles(depth))


def sides(own_ref, eo_ref, ee_ref, t):
    flip = odd("tx")
    a, b = eo_ref[t], ee_ref[t]
    return jnp.where(flip, b, a), own_ref[t], jnp.where(flip, a, b)


def corner_kernel(own_ref, eo_ref, ee_ref, up_ref, down_ref):
    sub = subs()
    west, _, east = sides(own_ref, eo_ref, ee_ref, 2 * FIELDS)
    wet = wet_tiles(west)[1], wet_tiles(east)[0]

    def edge(f):
        if f < 0:
            return [jnp.zeros(TILE, jnp.float32)] * 2
        if f == WET:
            w, e = wet
        else:
            w = sides(own_ref, eo_ref, ee_ref, 2 * f + 1)[0]
            e = sides(own_ref, eo_ref, ee_ref, 2 * f)[2]
        return [mix(w, half_turn(e)), mix(half_turn(w), e)]

    for k in range(PAIRS):
        a, b, c, d = edge(2 * k - 1) + edge(2 * k)
        turned = pltpu.roll(c, 4, 0)
        up_ref[k] = jnp.where(
            sub < 4,
            jnp.where(sub < 2, a, pltpu.roll(b, 2, 0)),
            jnp.where(sub < 6, turned, pltpu.roll(d, 6, 0)),
        )
        down_ref[k] = jnp.where(
            sub < 4,
            jnp.where(sub < 2, pltpu.roll(d, 2, 0), turned),
            jnp.where(sub < 6, pltpu.roll(b, 6, 0), a),
        )


def save(ref, tiles):
    for i, x in enumerate(tiles):
        ref[i] = x


def load(ref, *names):
    if not names:
        return [ref[i] for i in range(ref.shape[0])]
    return [[ref[2 * AUX.index(n)], ref[2 * AUX.index(n) + 1]] for n in names]


def own_kernel(
    own_ref, eo_ref, ee_ref, below_ref, above_ref, stoich_ref, raw_ref, part_ref, q1_ref,
    aux_ref, fc_ref, fr_ref, g_ref,
):
    def arrange(a, b):
        pairs = ((a[0], b[1]), (b[0], a[2]), (a[1], b[2]))
        out = []
        for low, high in pairs:
            out += [mix(low, half_turn(high)), mix(half_turn(low), high)]
        return out

    def wide(f):
        return arrange(*[sides(own_ref, eo_ref, ee_ref, 2 * f + i) for i in range(2)])

    def halo(f):
        return unstrip(below_ref[f], above_ref[f])

    u_w, v_w, t_w = [wide(f) for f in (U, V, T)]
    depth = sides(own_ref, eo_ref, ee_ref, 2 * FIELDS)
    w_w = arrange(*zip(*[wet_tiles(x) for x in depth]))
    u_h, v_h, t_h, w_h = [halo(f) for f in (U, V, T, WET)]
    u_s, v_s, t_s, w_s = [own_of(x) for x in (u_w, v_w, t_w, w_w)]
    w_e = edge_of(w_w)
    for f, wd, h in ((U, u_w, u_h), (V, v_w, v_h), (T, t_w, t_h), (WET, w_w, w_h)):
        save(raw_ref.at[f], edge_of(wd) + h)

    press = [0.05 * s for s in level_sum(t_w + t_h, True)]
    p_w, p_h = press[:6], press[6:]
    p_s = own_of(p_w)
    q_w, q_h = wide(2), halo(2)
    sun, heat = optics(own_of(q_w) + edge_of(q_w) + q_h, w_s + w_e + w_h)
    u1_w = east_speed(u_w, v_w, next_col(p_w), prev_col(p_w), w_w)
    (n_s, n_h), (b_s, b_h) = next_row(p_s, p_h), prev_row(p_s, p_h)
    v1_s = north_speed(u_s, v_s, n_s, b_s, w_s)
    v1_h = north_speed(u_h, v_h, n_h, b_h, w_h)
    (n_s, n_h), (b_s, b_h) = next_row(t_s, t_h), prev_row(t_s, t_h)
    around = plus(next_col(t_w), prev_col(t_w))
    t1_s = warmed(t_s, heat[:2], plus(n_s, b_s), own_of(around), w_s)
    save(fc_ref, col_factor(u1_w, w_w))
    fr_s, fr_h = row_factor(v1_s, v1_h, w_s, w_h)
    save(fr_ref, fr_s + fr_h)

    def advect(f):
        q_w, q_h = wide(f), halo(f)
        q_s, q_e = own_of(q_w), edge_of(q_w)
        col = col_divergence(q_w, load(fc_ref))
        fr = load(fr_ref)
        r_s, r_h = row_divergence(q_s, q_h, fr[:2], fr[2:])
        save(raw_ref.at[f], q_e + q_h)
        save(part_ref.at[f], minus(q_e, edge_of(col)) + minus(q_h, r_h))
        return minus(minus(q_s, own_of(col)), r_s)

    first = [advect(f) for f in range(5)]
    gain, chloro = [], []
    for i in range(2):
        core, g = reaction([first[f][i] for f in range(5)], sun[i], t1_s[i])
        gain.append(g)
        for f in range(5):
            q1_ref[f, i] = (first[f][i] + 0.2 * core[f]) * w_s[i]
        chloro.append((first[2][i] + 0.2 * core[2]) * w_s[i])
    sun2, heat2 = optics(chloro, w_s)
    save(g_ref, gain + w_s)
    values = dict(
        w_s=w_s, p_e=edge_of(p_w), p_h=p_h, sun_e=sun[2:4], sun_h=sun[4:], heat_e=heat[2:4],
        heat_h=heat[4:], cols_e=edge_of(around), rows_h=plus(n_h, b_h), u1_s=own_of(u1_w),
        u1_e=edge_of(u1_w), v1_s=v1_s, v1_h=v1_h, t1_s=t1_s, sun2=sun2, heat2=heat2,
    )
    save(aux_ref, [x for n in AUX for x in values[n]])

    def others(f, _):
        s = stoich_ref[f - 5]
        k = load(g_ref)
        out = each(lambda a, g, w: (a + s * g) * w, advect(f), k[:2], k[2:])
        save(q1_ref.at[f], out)
        return 0

    lax.fori_loop(5, NTR, others, 0, unroll=2)


def plain(x):
    return [mix(x[0], half_turn(x[1])), mix(half_turn(x[0]), x[1])]


def edge_kernel(
    raw_ref, part_ref, aux_ref, below_ref, above_ref, stoich_ref, ocean_ref, q_ref, c2_ref,
    r2_ref, t2_ref, fc_ref, fr_ref, g_ref,
):
    sub4 = subs() < 4

    def corners(k):
        b, a = below_ref[k], above_ref[k]
        return (
            [
                jnp.where(sub4, b, a),
                jnp.where(sub4, pltpu.roll(b, 6, 0), pltpu.roll(a, 2, 0)),
            ],
            [
                pltpu.roll(jnp.where(sub4, a, b), 4, 0),
                jnp.where(sub4, pltpu.roll(b, 2, 0), pltpu.roll(a, 6, 0)),
            ],
        )

    def raw(f):
        x = load(raw_ref.at[f])
        return x[:2], x[2:]

    (u_c, v_c), (t_c, w_c) = corners((U + 1) // 2), corners((T + 1) // 2)
    (u_e, u_h), (v_e, v_h), (t_e, t_h), (w_e, w_h) = [raw(f) for f in (U, V, T, WET)]
    w_s, p_e, p_h = load(aux_ref, "w_s", "p_e", "p_h")
    p_c = [0.05 * s for s in level_sum(t_c, True)]

    (n_h, n_c), (b_h, b_c) = next_split(p_h, p_c), prev_split(p_h, p_c)
    u1_h = east_speed(u_h, v_h, n_h, b_h, w_h)
    u1_c = east_speed(u_c, v_c, n_c, b_c, w_c)
    (n_e, n_c), (b_e, b_c) = next_row(p_e, p_c), prev_row(p_e, p_c)
    v1_e = north_speed(u_e, v_e, n_e, b_e, w_e)
    v1_c = north_speed(u_c, v_c, n_c, b_c, w_c)
    heat_e, heat_h, cols_e, rows_h = load(aux_ref, "heat_e", "heat_h", "cols_e", "rows_h")
    rows_e = plus(next_row(t_e, t_c)[0], prev_row(t_e, t_c)[0])
    t1_e = warmed(t_e, heat_e, rows_e, cols_e, w_e)
    cols_h = plus(next_split(t_h, t_c)[0], prev_split(t_h, t_c)[0])
    t1_h = warmed(t_h, heat_h, rows_h, cols_h, w_h)
    fc_h, fc_c = split_factor(u1_h, u1_c, w_h, w_c)
    save(fc_ref, fc_h + fc_c)
    fr_e, fr_c = row_factor(v1_e, v1_c, w_e, w_c)
    save(fr_ref, fr_e + fr_c)

    def advect1(f, q_c):
        q_e, q_h = raw(f)
        fc, fr = load(fc_ref), load(fr_ref)
        row = row_divergence(q_e, q_c, fr[:2], fr[2:])[0]
        col = split_divergence(q_h, q_c, fc[:2], fc[2:])
        return minus(load(part_ref.at[f]), row + col)

    c = [corners(k) for k in range(3)]
    core_corners = [c[0][1], c[1][0], c[1][1], c[2][0], c[2][1]]
    first = [advect1(f, core_corners[f]) for f in range(5)]
    sun_e, sun_h = load(aux_ref, "sun_e", "sun_h")
    w_four, sun, t1_four, gain = w_e + w_h, sun_e + sun_h, t1_e + t1_h, []
    for i in range(4):
        core, g = reaction([first[f][i] for f in range(5)], sun[i], t1_four[i])
        gain.append(g)
        for f in range(5):
            q_ref[f, i] = (first[f][i] + 0.2 * core[f]) * w_four[i]
    save(g_ref, gain + w_four)

    def others1(k, _):
        both = corners(k)
        for j in range(2):
            f = 2 * k - 1 + j
            s = stoich_ref[f - 5]
            g = load(g_ref)
            out = each(lambda a, g, w: (a + s * g) * w, advect1(f, both[j]), g[:4], g[4:])
            save(q_ref.at[f], out)
        return 0

    lax.fori_loop(3, 10, others1, 0)

    u1_s, u1_e, v1_s, v1_h, t1_s, _, heat2 = load(
        aux_ref, "u1_s", "u1_e", "v1_s", "v1_h", "t1_s", "sun2", "heat2"
    )
    p1 = [0.05 * s for s in level_sum(t1_s + t1_e + t1_h, True)]
    p_s, p_e, p_h = p1[:2], p1[2:4], p1[4:]
    (n_s, n_e), (b_s, b_e) = next_split(p_s, p_e), prev_split(p_s, p_e)
    u2_s = east_speed(u1_s, v1_s, n_s, b_s, w_s)
    u2_e = east_speed(u1_e, v1_e, n_e, b_e, w_e)
    (n_s, n_h), (b_s, b_h) = next_row(p_s, p_h), prev_row(p_s, p_h)
    v2_s = north_speed(u1_s, v1_s, n_s, b_s, w_s)
    v2_h = north_speed(u1_h, v1_h, n_h, b_h, w_h)
    rows = plus(next_row(t1_s, t1_h)[0], prev_row(t1_s, t1_h)[0])
    cols = plus(next_split(t1_s, t1_e)[0], prev_split(t1_s, t1_e)[0])
    t2 = warmed(t1_s, heat2, rows, cols, w_s)

    save(t2_ref, t2)
    for k, x in enumerate((u2_s, v2_s, t2)):
        for i, tile in enumerate(plain(x)):
            for peer in range(ocean_ref.shape[0]):
                ocean_ref[peer, k, :, 128 * i : 128 * (i + 1)] = tile

    fc_s, fc_e = split_factor(u2_s, u2_e, w_s, w_e)
    save(c2_ref, fc_s + fc_e)
    fr_s, fr_h = row_factor(v2_s, v2_h, w_s, w_h)
    save(r2_ref, fr_s + fr_h)


def last_kernel(
    q1_ref, aux_ref, q_ref, c2_ref, r2_ref, t2_ref, stoich_ref, out_ref, g2_ref
):
    w_s, sun2 = load(aux_ref, "w_s", "sun2")
    t2 = load(t2_ref)

    def advect2(f):
        q_s, x = load(q1_ref.at[f]), load(q_ref.at[f])
        fc, fr = load(c2_ref), load(r2_ref)
        row = row_divergence(q_s, x[2:], fr[:2], fr[2:])[0]
        return minus(minus(q_s, split_divergence(q_s, x[:2], fc[:2], fc[2:])), row)

    def finish(f, tiles):
        for i, x in enumerate(plain(tiles)):
            out_ref[f, 0, :, 128 * i : 128 * (i + 1)] = x

    first = [advect2(f) for f in range(5)]
    done = [[] for _ in range(5)]
    gain = []
    for i in range(2):
        core, g = reaction([first[f][i] for f in range(5)], sun2[i], t2[i])
        gain.append(g)
        for f in range(5):
            done[f].append((first[f][i] + 0.2 * core[f]) * w_s[i])
    for f in range(5):
        finish(f, done[f])
    save(g2_ref, gain + w_s)

    def others2(f, _):
        s = stoich_ref[f - 5]
        k = load(g2_ref)
        finish(f, each(lambda a, g, w: (a + s * g) * w, advect2(f), k[:2], k[2:]))
        return 0

    lax.fori_loop(5, NTR, others2, 0, unroll=2)


def swaps(count, first, place=lambda i: i):
    pairs = []
    for a in range(first, count - 1, 2):
        pairs += [(place(a), place(a + 1)), (place(a + 1), place(a))]
    return pairs


def shards(ocean, tracers, bottom, stoich):
    comps = lax.axis_size("comp")
    bands = lax.axis_size("ty")
    tiles = lax.axis_size("tx")
    vmem = pl.BlockSpec(memory_space=VMEM)

    def arr(*dims):
        return VMEM(dims, jnp.float32)

    def near(*args):
        return [pltpu.with_memory_space_constraint(a, VMEM) for a in args]

    def place(row):
        return (row % comps) * bands + row // comps

    axes = ("comp", "ty")
    count = comps * bands
    ups = [(place(r), place(r - 1)) for r in range(1, count)]
    downs = [(b, a) for a, b in ups]

    def kernel(body, outs, ins, scratch=(), scalars=False):
        return pl.pallas_call(
            body,
            out_shape=tuple(outs),
            in_specs=[vmem] * ins + [pl.BlockSpec(memory_space=pltpu.SMEM)] * scalars,
            out_specs=(vmem,) * len(outs),
            scratch_shapes=[VMEM((*n, *TILE), jnp.float32) for n in scratch],
        )

    packed, strip_up, strip_down, yields = kernel(
        pack_kernel,
        [arr(n, *TILE) for n in (2 * FIELDS + 1, FIELDS + 1, FIELDS + 1, NTR - 5)],
        3,
        scalars=True,
    )(ocean, tracers, bottom.T, stoich)
    from_odd = lax.ppermute(packed, "tx", swaps(tiles, 1))
    from_even = lax.ppermute(packed, "tx", swaps(tiles, 0))
    below = lax.ppermute(strip_up, axes, ups)
    above = lax.ppermute(strip_down, axes, downs)
    blocks = near(packed, from_odd, from_even)
    corner_up, corner_down = kernel(
        corner_kernel, [arr(PAIRS, *TILE), arr(PAIRS, *TILE)], 3
    )(*blocks)
    corner_below = lax.ppermute(corner_up, axes, ups)
    corner_above = lax.ppermute(corner_down, axes, downs)
    state = kernel(
        own_kernel,
        [
            arr(FIELDS + 1, 4, *TILE),
            arr(NTR, 4, *TILE),
            arr(NTR, 2, *TILE),
            arr(2 * len(AUX), *TILE),
        ],
        6,
        [(6,), (4,), (4,)],
    )(*blocks, *near(below, above, yields))
    raw, part, q1_own, aux = near(*state)
    rows, *rest = kernel(
        edge_kernel,
        [arr(comps, 3, ROWS, 256), arr(NTR, 4, *TILE)] + [arr(n, *TILE) for n in (4, 4, 2)],
        6,
        [(4,), (4,), (8,)],
    )(raw, part, aux, *near(corner_below, corner_above, yields))
    gathered = lax.all_to_all(rows, "comp", 0, 0, tiled=True)
    (tracers_out,) = kernel(
        last_kernel, [jax.ShapeDtypeStruct((NTR, 1, ROWS, 256), jnp.float32)], 7, [(4,)]
    )(q1_own, aux, *near(*rest, yields))
    return jnp.swapaxes(gathered, 0, 1).reshape(3, comps * ROWS, 256), tracers_out


def solution(mesh):
    in_specs = (P(None, "ty", "tx"), P(None, "ty", "comp", "tx"), P("ty", "tx"), P())
    out_specs = (P(None, "ty", "tx"), P(None, "ty", "comp", "tx"))
    return jax.shard_map(shards, mesh=mesh, in_specs=in_specs, out_specs=out_specs, check_vma=False)
```

```python
import jax
import jax.numpy as jnp
from jax import lax
from jax.experimental import pallas as pl
from jax.experimental.pallas import tpu as pltpu
from jax.sharding import PartitionSpec as P


LEV = 64
NTR = 19
ROWS = 8
FIELDS = 22
U, V, T, WET = 19, 20, 21, 22
PAIRS = 12
AUX = (
    "w_s", "p_e", "p_h", "sun_e", "sun_h", "heat_e", "heat_h", "cols_e", "rows_h", "u1_s",
    "u1_e", "v1_s", "v1_h", "t1_s", "sun2", "heat2",
)
VMEM = pltpu.VMEM
TILE = (ROWS, 128)


def lanes():
    return lax.broadcasted_iota(jnp.int32, TILE, 1)


def subs():
    return lax.broadcasted_iota(jnp.int32, TILE, 0)


def half_turn(x):
    return pltpu.roll(x, LEV, 1)


def mix(a, b):
    return jnp.where(lanes() < LEV, a, b)


def own_of(w):
    return [mix(w[4], w[0]), mix(w[5], w[1])]


def edge_of(w):
    return [w[2], w[3]]


def each(f, *lists):
    return [f(*args) for args in zip(*lists)]


def next_col(x):
    return x[1:] + [half_turn(x[0])]


def prev_col(x):
    return [half_turn(x[-1])] + x[:-1]


def next_split(s, e):
    return [s[1], mix(half_turn(s[0]), e[0])], [e[1], s[0]]


def prev_split(s, e):
    return [mix(e[1], half_turn(s[1])), s[0]], [s[1], e[0]]


def next_row(o, h):
    edge = subs() == 0
    return (
        [pltpu.roll(jnp.where(edge, b, a), ROWS - 1, 0) for a, b in zip(o, h)],
        [pltpu.roll(jnp.where(edge, a, b), ROWS - 1, 0) for a, b in zip(o, h)],
    )


def prev_row(o, h):
    edge = subs() == ROWS - 1
    return (
        [pltpu.roll(jnp.where(edge, b, a), 1, 0) for a, b in zip(o, h)],
        [pltpu.roll(jnp.where(edge, a, b), 1, 0) for a, b in zip(o, h)],
    )


def minmod(a, b):
    return jnp.maximum(jnp.minimum(a, b), jnp.minimum(jnp.maximum(a, b), 0.0))


def upwind(fac, left, right):
    return fac * jnp.where(fac > 0.0, left, right)


def minus(x, y):
    return each(lambda a, b: a - b, x, y)


def col_divergence(q, fac):
    d = minus(next_col(q), q)
    m = each(minmod, d, prev_col(d))
    left = each(lambda a, b: (a + a) + b, q, m)
    right = each(lambda a, b: (a + a) - b, q, m)
    flux = each(upwind, fac, left, next_col(right))
    return minus(flux, prev_col(flux))


def split_divergence(s, e, fac_s, fac_e):
    n_s, n_e = next_split(s, e)
    d_s, d_e = minus(n_s, s), minus(n_e, e)
    b_s, b_e = prev_split(d_s, d_e)
    m_s, m_e = each(minmod, d_s, b_s), each(minmod, d_e, b_e)
    r_s = each(lambda a, b: (a + a) - b, s, m_s)
    r_e = each(lambda a, b: (a + a) - b, e, m_e)
    n_s, n_e = next_split(r_s, r_e)
    f_s = each(lambda f, a, b, c: upwind(f, (a + a) + b, c), fac_s, s, m_s, n_s)
    f_e = each(lambda f, a, b, c: upwind(f, (a + a) + b, c), fac_e, e, m_e, n_e)
    return minus(f_s, prev_split(f_s, f_e)[0])


def row_divergence(o, h, fac_o, fac_h):
    n_o, n_h = next_row(o, h)
    d_o, d_h = minus(n_o, o), minus(n_h, h)
    b_o, b_h = prev_row(d_o, d_h)
    m_o, m_h = each(minmod, d_o, b_o), each(minmod, d_h, b_h)
    r_o = each(lambda a, b: (a + a) - b, o, m_o)
    r_h = each(lambda a, b: (a + a) - b, h, m_h)
    n_o, n_h = next_row(r_o, r_h)
    f_o = each(lambda f, a, b, c: upwind(f, (a + a) + b, c), fac_o, o, m_o, n_o)
    f_h = each(lambda f, a, b, c: upwind(f, (a + a) + b, c), fac_h, h, m_h, n_h)
    p_o, p_h = prev_row(f_o, f_h)
    return minus(f_o, p_o), minus(f_h, p_h)


def half_factor(vel, wet, next_vel, next_wet):
    return 0.5 * (0.08 * (0.5 * (vel + next_vel) * wet * next_wet))


def col_factor(vel, wet):
    return each(half_factor, vel, wet, next_col(vel), next_col(wet))


def split_factor(vel_s, vel_e, wet_s, wet_e):
    n_s, n_e = next_split(vel_s, vel_e)
    w_s, w_e = next_split(wet_s, wet_e)
    return each(half_factor, vel_s, wet_s, n_s, w_s), each(half_factor, vel_e, wet_e, n_e, w_e)


def row_factor(vel_o, vel_h, wet_o, wet_h):
    n_o, n_h = next_row(vel_o, vel_h)
    w_o, w_h = next_row(wet_o, wet_h)
    return each(half_factor, vel_o, wet_o, n_o, w_o), each(half_factor, vel_h, wet_h, n_h, w_h)


def level_sum(tiles, inclusive):
    r = lax.rem(lax.broadcasted_iota(jnp.int32, (256, 128), 0), 128)
    c = lax.broadcasted_iota(jnp.int32, (256, 128), 1)
    above = (r <= c) if inclusive else (r < c)
    ladder = jnp.where(((r < LEV) == (c < LEV)) & above, 1.0, 0.0).astype(jnp.bfloat16)
    x = jnp.concatenate(tiles, axis=0)
    major = x.astype(jnp.bfloat16)
    minor = (x - major.astype(jnp.float32)).astype(jnp.bfloat16)
    out = jnp.dot(
        jnp.concatenate([major, minor], axis=1), ladder, preferred_element_type=jnp.float32
    )
    return [out[ROWS * i : ROWS * (i + 1)] for i in range(len(tiles))]


def optics(chloro, wet):
    absorb = each(lambda a, w: (0.04 + 0.03 * jnp.maximum(a, 0.0)) * w, chloro, wet)
    sun = [jnp.exp(-s) for s in level_sum(absorb, False)]
    heat = each(lambda s, a, w: s * (1.0 - jnp.exp(-a)) * w, sun, absorb, wet)
    return sun, heat


def east_speed(u, v, n, b, w):
    return each(
        lambda u, v, n, b, w: w * (0.95 * u + 0.2 * (v - 0.5 * (n - b))), u, v, n, b, w
    )


def north_speed(u, v, n, b, w):
    return each(
        lambda u, v, n, b, w: w * (0.95 * v - 0.2 * (u + 0.5 * (n - b))), u, v, n, b, w
    )


def plus(x, y):
    return each(lambda a, b: a + b, x, y)


def warmed(t, heat, rows, cols, w):
    return each(
        lambda t, heat, r, c, w: w * (t + 0.2 * (2.0 * heat + 0.2 * (r + c - 4.0 * t))),
        t, heat, rows, cols, w,
    )


def reaction(adv, sun, temp):
    n, p, c, z, d = [jnp.maximum(a, 0.0) for a in adv]
    uptake = sun / (sun + 0.2) * n / (n + 0.5) * jnp.exp(0.1 * temp)
    growth = uptake * p
    grazing = 0.8 * z * p * p / (p * p + 0.3)
    dying = 0.1 * p
    remin = 0.2 * d
    core = [
        remin - growth,
        growth - grazing - dying,
        0.3 * (0.5 * p - c) + 0.2 * growth,
        0.3 * grazing - 0.05 * z,
        dying + 0.7 * grazing + 0.05 * z - remin,
    ]
    return core, 0.2 * (growth - remin)


def odd(name):
    return lax.rem(lax.axis_index(name), 2) == 1


def wet_tiles(depth):
    level = lax.rem(lanes(), LEV).astype(jnp.float32)
    return [
        jnp.where(level < mix(depth[:, c : c + 1], depth[:, c + 1 : c + 2]), 1.0, 0.0)
        for c in (0, 2)
    ]


def middle():
    return (subs() >= 2) & (subs() < 6)


def pack_kernel(
    ocean_ref, tr_ref, bot_ref, stoich_ref, out_ref, first_ref, rest_ref, yield_ref
):
    for j in range(NTR - 5):
        yield_ref[j] = jnp.full(TILE, stoich_ref[j], jnp.float32)
    start = pl.multiple_of(lax.axis_index("comp") * ROWS, ROWS)
    rows = pl.ds(start, ROWS)
    band = bot_ref.shape[1]
    row = lax.broadcasted_iota(jnp.int32, (ROWS, band), 0) + start
    pick = row == lax.broadcasted_iota(jnp.int32, (ROWS, band), 1)
    depth = jnp.zeros(TILE, jnp.float32)
    for c in range(4):
        line = bot_ref[c : c + 1, :].astype(jnp.float32)
        depth = jnp.where(
            lanes() == c, jnp.sum(jnp.where(pick, line, 0.0), axis=1, keepdims=True), depth
        )
    out_ref[2 * FIELDS] = depth
    rest_ref[PAIRS + FIELDS] = depth
    flip = odd("tx")
    wet = wet_tiles(depth)

    def near_tile(f):
        if f < 0:
            return jnp.zeros(TILE, jnp.float32)
        if f == WET:
            return jnp.where(flip, wet[1], wet[0])
        x = tr_ref[f, 0] if f < NTR else ocean_ref[f - NTR, rows, :]
        a, b = x[:, :128], x[:, 128:]
        out_ref[2 * f] = a
        out_ref[2 * f + 1] = b
        rest_ref[PAIRS + f] = jnp.where(flip, a, b)
        return jnp.where(flip, b, a)

    for k in range(PAIRS):
        x, y = near_tile(2 * k - 1), pltpu.roll(near_tile(2 * k), 4, 0)
        first_ref[k] = jnp.where(middle(), y, x)
        rest_ref[k] = jnp.where(middle(), x, y)


def row_kernel(own_ref, chip_ref, ca_ref, cb_ref, up_ref, down_ref, first_ref):
    flip = odd("tx")
    sub = subs()
    upper = sub < 4

    def strip(f, a, b):
        a, b = mix(a, half_turn(b)), pltpu.roll(mix(half_turn(a), b), 4, 0)
        up_ref[f] = jnp.where(upper, a, b)
        down_ref[f] = jnp.where(upper, b, a)

    for f in range(FIELDS):
        strip(f, own_ref[2 * f], own_ref[2 * f + 1])
    strip(WET, *wet_tiles(own_ref[2 * FIELDS]))
    wet = wet_tiles(chip_ref[2 * FIELDS])

    def edge(f, far):
        if f < 0:
            return [far, far]
        west, east = wet if f == WET else (chip_ref[2 * f], chip_ref[2 * f + 1])
        w = jnp.where(flip, east, far)
        e = jnp.where(flip, far, west)
        return [mix(w, half_turn(e)), mix(half_turn(w), e)]

    for k in range(PAIRS):
        far = ca_ref[k] + cb_ref[k]
        first_ref[k] = far
        a, b, c, d = edge(2 * k - 1, far) + edge(2 * k, pltpu.roll(far, 4, 0))
        turned = pltpu.roll(c, 4, 0)
        up_ref[WET + 1 + k] = jnp.where(
            upper,
            jnp.where(sub < 2, a, pltpu.roll(b, 2, 0)),
            jnp.where(sub < 6, turned, pltpu.roll(d, 6, 0)),
        )
        down_ref[WET + 1 + k] = jnp.where(
            upper,
            jnp.where(sub < 2, pltpu.roll(d, 2, 0), turned),
            jnp.where(sub < 6, pltpu.roll(b, 6, 0), a),
        )


def save(ref, tiles):
    for i, x in enumerate(tiles):
        ref[i] = x


def load(ref, *names):
    if not names:
        return [ref[i] for i in range(ref.shape[0])]
    return [[ref[2 * AUX.index(n)], ref[2 * AUX.index(n) + 1]] for n in names]


def own_kernel(
    own_ref, chip_ref, first_ref, ra_ref, rb_ref, te_ref, to_ref, stoich_ref, raw_ref, part_ref,
    q1_ref, aux_ref, near_ref, fc_ref, fr_ref, g_ref,
):
    flip = odd("tx")
    even = jnp.logical_not(odd("comp"))
    mid = middle()
    for k in range(PAIRS):
        c, r = first_ref[k], ra_ref[k] + rb_ref[k]
        if k:
            near_ref[2 * k - 1] = jnp.where(mid, r, c)
        near_ref[2 * k] = pltpu.roll(jnp.where(mid, c, r), 4, 0)

    def arrange(a, b):
        pairs = ((a[0], b[1]), (b[0], a[2]), (a[1], b[2]))
        out = []
        for low, high in pairs:
            out += [mix(low, half_turn(high)), mix(half_turn(low), high)]
        return out

    def blocks(f):
        n, d = near_ref[f], ra_ref[PAIRS + f] + rb_ref[PAIRS + f]
        c0, c1 = chip_ref[2 * f], chip_ref[2 * f + 1]
        west = jnp.where(flip, c0, d), jnp.where(flip, c1, n)
        east = jnp.where(flip, n, c0), jnp.where(flip, d, c1)
        return west, (own_ref[2 * f], own_ref[2 * f + 1]), east

    def wide(f):
        return arrange(*zip(*blocks(f)))

    def halo(f):
        first = (subs() < 4) == even
        te, to = te_ref[f], to_ref[f]
        return [jnp.where(first, te, to), pltpu.roll(jnp.where(first, to, te), 4, 0)]

    u_w, v_w, t_w = [wide(f) for f in (U, V, T)]
    far = wet_tiles(ra_ref[PAIRS + FIELDS] + rb_ref[PAIRS + FIELDS])
    close = wet_tiles(chip_ref[2 * FIELDS])
    own = wet_tiles(own_ref[2 * FIELDS])
    west = [jnp.where(flip, c, d) for c, d in zip(close, far)]
    east = [jnp.where(flip, d, c) for c, d in zip(close, far)]
    w_w = arrange(*zip(west, own, east))
    u_h, v_h, t_h, w_h = [halo(f) for f in (U, V, T, WET)]
    u_s, v_s, t_s, w_s = [own_of(x) for x in (u_w, v_w, t_w, w_w)]
    w_e = edge_of(w_w)
    for f, wd, h in ((U, u_w, u_h), (V, v_w, v_h), (T, t_w, t_h), (WET, w_w, w_h)):
        save(raw_ref.at[f], edge_of(wd) + h)

    press = [0.05 * s for s in level_sum(t_w + t_h, True)]
    p_w, p_h = press[:6], press[6:]
    p_s = own_of(p_w)
    q_w, q_h = wide(2), halo(2)
    sun, heat = optics(own_of(q_w) + edge_of(q_w) + q_h, w_s + w_e + w_h)
    u1_w = east_speed(u_w, v_w, next_col(p_w), prev_col(p_w), w_w)
    (n_s, n_h), (b_s, b_h) = next_row(p_s, p_h), prev_row(p_s, p_h)
    v1_s = north_speed(u_s, v_s, n_s, b_s, w_s)
    v1_h = north_speed(u_h, v_h, n_h, b_h, w_h)
    (n_s, n_h), (b_s, b_h) = next_row(t_s, t_h), prev_row(t_s, t_h)
    around = plus(next_col(t_w), prev_col(t_w))
    t1_s = warmed(t_s, heat[:2], plus(n_s, b_s), own_of(around), w_s)
    save(fc_ref, col_factor(u1_w, w_w))
    fr_s, fr_h = row_factor(v1_s, v1_h, w_s, w_h)
    save(fr_ref, fr_s + fr_h)

    def advect(f):
        q_w, q_h = wide(f), halo(f)
        q_s, q_e = own_of(q_w), edge_of(q_w)
        col = col_divergence(q_w, load(fc_ref))
        fr = load(fr_ref)
        r_s, r_h = row_divergence(q_s, q_h, fr[:2], fr[2:])
        save(raw_ref.at[f], q_e + q_h)
        save(part_ref.at[f], minus(q_e, edge_of(col)) + minus(q_h, r_h))
        return minus(minus(q_s, own_of(col)), r_s)

    first = [advect(f) for f in range(5)]
    gain, chloro = [], []
    for i in range(2):
        core, g = reaction([first[f][i] for f in range(5)], sun[i], t1_s[i])
        gain.append(g)
        for f in range(5):
            q1_ref[f, i] = (first[f][i] + 0.2 * core[f]) * w_s[i]
        chloro.append((first[2][i] + 0.2 * core[2]) * w_s[i])
    sun2, heat2 = optics(chloro, w_s)
    save(g_ref, gain + w_s)
    values = dict(
        w_s=w_s, p_e=edge_of(p_w), p_h=p_h, sun_e=sun[2:4], sun_h=sun[4:], heat_e=heat[2:4],
        heat_h=heat[4:], cols_e=edge_of(around), rows_h=plus(n_h, b_h), u1_s=own_of(u1_w),
        u1_e=edge_of(u1_w), v1_s=v1_s, v1_h=v1_h, t1_s=t1_s, sun2=sun2, heat2=heat2,
    )
    save(aux_ref, [x for n in AUX for x in values[n]])

    def others(f, _):
        s = stoich_ref[f - 5]
        k = load(g_ref)
        out = each(lambda a, g, w: (a + s * g) * w, advect(f), k[:2], k[2:])
        save(q1_ref.at[f], out)
        return 0

    lax.fori_loop(5, NTR, others, 0, unroll=2)


def plain(x):
    return [mix(x[0], half_turn(x[1])), mix(half_turn(x[0]), x[1])]


def edge_kernel(
    raw_ref, part_ref, aux_ref, te_ref, to_ref, stoich_ref, ocean_ref, q_ref, c2_ref,
    r2_ref, t2_ref, fc_ref, fr_ref, g_ref,
):
    sub4 = subs() < 4
    swapped = odd("comp")

    def corners(k):
        te, to = te_ref[WET + 1 + k], to_ref[WET + 1 + k]
        b, a = jnp.where(swapped, to, te), jnp.where(swapped, te, to)
        return (
            [
                jnp.where(sub4, b, a),
                jnp.where(sub4, pltpu.roll(b, 6, 0), pltpu.roll(a, 2, 0)),
            ],
            [
                pltpu.roll(jnp.where(sub4, a, b), 4, 0),
                jnp.where(sub4, pltpu.roll(b, 2, 0), pltpu.roll(a, 6, 0)),
            ],
        )

    def raw(f):
        x = load(raw_ref.at[f])
        return x[:2], x[2:]

    (u_c, v_c), (t_c, w_c) = corners((U + 1) // 2), corners((T + 1) // 2)
    (u_e, u_h), (v_e, v_h), (t_e, t_h), (w_e, w_h) = [raw(f) for f in (U, V, T, WET)]
    w_s, p_e, p_h = load(aux_ref, "w_s", "p_e", "p_h")
    p_c = [0.05 * s for s in level_sum(t_c, True)]

    (n_h, n_c), (b_h, b_c) = next_split(p_h, p_c), prev_split(p_h, p_c)
    u1_h = east_speed(u_h, v_h, n_h, b_h, w_h)
    u1_c = east_speed(u_c, v_c, n_c, b_c, w_c)
    (n_e, n_c), (b_e, b_c) = next_row(p_e, p_c), prev_row(p_e, p_c)
    v1_e = north_speed(u_e, v_e, n_e, b_e, w_e)
    v1_c = north_speed(u_c, v_c, n_c, b_c, w_c)
    heat_e, heat_h, cols_e, rows_h = load(aux_ref, "heat_e", "heat_h", "cols_e", "rows_h")
    rows_e = plus(next_row(t_e, t_c)[0], prev_row(t_e, t_c)[0])
    t1_e = warmed(t_e, heat_e, rows_e, cols_e, w_e)
    cols_h = plus(next_split(t_h, t_c)[0], prev_split(t_h, t_c)[0])
    t1_h = warmed(t_h, heat_h, rows_h, cols_h, w_h)
    fc_h, fc_c = split_factor(u1_h, u1_c, w_h, w_c)
    save(fc_ref, fc_h + fc_c)
    fr_e, fr_c = row_factor(v1_e, v1_c, w_e, w_c)
    save(fr_ref, fr_e + fr_c)

    def advect1(f, q_c):
        q_e, q_h = raw(f)
        fc, fr = load(fc_ref), load(fr_ref)
        row = row_divergence(q_e, q_c, fr[:2], fr[2:])[0]
        col = split_divergence(q_h, q_c, fc[:2], fc[2:])
        return minus(load(part_ref.at[f]), row + col)

    c = [corners(k) for k in range(3)]
    core_corners = [c[0][1], c[1][0], c[1][1], c[2][0], c[2][1]]
    first = [advect1(f, core_corners[f]) for f in range(5)]
    sun_e, sun_h = load(aux_ref, "sun_e", "sun_h")
    w_four, sun, t1_four, gain = w_e + w_h, sun_e + sun_h, t1_e + t1_h, []
    for i in range(4):
        core, g = reaction([first[f][i] for f in range(5)], sun[i], t1_four[i])
        gain.append(g)
        for f in range(5):
            q_ref[f, i] = (first[f][i] + 0.2 * core[f]) * w_four[i]
    save(g_ref, gain + w_four)

    def others1(k, _):
        both = corners(k)
        for j in range(2):
            f = 2 * k - 1 + j
            s = stoich_ref[f - 5]
            g = load(g_ref)
            out = each(lambda a, g, w: (a + s * g) * w, advect1(f, both[j]), g[:4], g[4:])
            save(q_ref.at[f], out)
        return 0

    lax.fori_loop(3, 10, others1, 0)

    u1_s, u1_e, v1_s, v1_h, t1_s, _, heat2 = load(
        aux_ref, "u1_s", "u1_e", "v1_s", "v1_h", "t1_s", "sun2", "heat2"
    )
    p1 = [0.05 * s for s in level_sum(t1_s + t1_e + t1_h, True)]
    p_s, p_e, p_h = p1[:2], p1[2:4], p1[4:]
    (n_s, n_e), (b_s, b_e) = next_split(p_s, p_e), prev_split(p_s, p_e)
    u2_s = east_speed(u1_s, v1_s, n_s, b_s, w_s)
    u2_e = east_speed(u1_e, v1_e, n_e, b_e, w_e)
    (n_s, n_h), (b_s, b_h) = next_row(p_s, p_h), prev_row(p_s, p_h)
    v2_s = north_speed(u1_s, v1_s, n_s, b_s, w_s)
    v2_h = north_speed(u1_h, v1_h, n_h, b_h, w_h)
    rows = plus(next_row(t1_s, t1_h)[0], prev_row(t1_s, t1_h)[0])
    cols = plus(next_split(t1_s, t1_e)[0], prev_split(t1_s, t1_e)[0])
    t2 = warmed(t1_s, heat2, rows, cols, w_s)

    save(t2_ref, t2)
    for k, x in enumerate((u2_s, v2_s, t2)):
        for i, tile in enumerate(plain(x)):
            for peer in range(ocean_ref.shape[0]):
                ocean_ref[peer, k, :, 128 * i : 128 * (i + 1)] = tile

    fc_s, fc_e = split_factor(u2_s, u2_e, w_s, w_e)
    save(c2_ref, fc_s + fc_e)
    fr_s, fr_h = row_factor(v2_s, v2_h, w_s, w_h)
    save(r2_ref, fr_s + fr_h)


def last_kernel(
    q1_ref, aux_ref, q_ref, c2_ref, r2_ref, t2_ref, stoich_ref, out_ref, g2_ref
):
    w_s, sun2 = load(aux_ref, "w_s", "sun2")
    t2 = load(t2_ref)

    def advect2(f):
        q_s, x = load(q1_ref.at[f]), load(q_ref.at[f])
        fc, fr = load(c2_ref), load(r2_ref)
        row = row_divergence(q_s, x[2:], fr[:2], fr[2:])[0]
        return minus(minus(q_s, split_divergence(q_s, x[:2], fc[:2], fc[2:])), row)

    def finish(f, tiles):
        for i, x in enumerate(plain(tiles)):
            out_ref[f, 0, :, 128 * i : 128 * (i + 1)] = x

    first = [advect2(f) for f in range(5)]
    done = [[] for _ in range(5)]
    gain = []
    for i in range(2):
        core, g = reaction([first[f][i] for f in range(5)], sun2[i], t2[i])
        gain.append(g)
        for f in range(5):
            done[f].append((first[f][i] + 0.2 * core[f]) * w_s[i])
    for f in range(5):
        finish(f, done[f])
    save(g2_ref, gain + w_s)

    def others2(f, _):
        s = stoich_ref[f - 5]
        k = load(g2_ref)
        finish(f, each(lambda a, g, w: (a + s * g) * w, advect2(f), k[:2], k[2:]))
        return 0

    lax.fori_loop(5, NTR, others2, 0, unroll=2)


def swaps(count, first, place=lambda i: i):
    pairs = []
    for a in range(first, count - 1, 2):
        pairs += [(place(a), place(a + 1)), (place(a + 1), place(a))]
    return pairs


def far_pairs(bands, tiles):
    group = 8
    length = bands * (tiles // group)

    def steps(tx, ty):
        z = tx // group * bands + ty
        return min(z, length - z)

    later, sooner = [], []
    for ty in range(bands):
        for a in range(1, tiles - 1, 2):
            pair = (ty * tiles + a, ty * tiles + a + 1)
            if steps(a, ty) < steps(a + 1, ty):
                pair = pair[::-1]
            later.append(pair)
            sooner.append(pair[::-1])
    return later, sooner


def shards(ocean, tracers, bottom, stoich):
    comps = lax.axis_size("comp")
    bands = lax.axis_size("ty")
    tiles = lax.axis_size("tx")
    vmem = pl.BlockSpec(memory_space=VMEM)

    def arr(*dims):
        return VMEM(dims, jnp.float32)

    def near(*args):
        return [pltpu.with_memory_space_constraint(a, VMEM) for a in args]

    def place(row):
        return (row % comps) * bands + row // comps

    axes = ("comp", "ty")
    count = comps * bands

    def kernel(body, outs, ins, scratch=(), scalars=False):
        return pl.pallas_call(
            body,
            out_shape=tuple(outs),
            in_specs=[vmem] * ins + [pl.BlockSpec(memory_space=pltpu.SMEM)] * scalars,
            out_specs=(vmem,) * len(outs),
            scratch_shapes=[VMEM((*n, *TILE), jnp.float32) for n in scratch],
        )

    packed, first, rest, yields = kernel(
        pack_kernel,
        [arr(n, *TILE) for n in (2 * FIELDS + 1, PAIRS, PAIRS + FIELDS + 1, NTR - 5)],
        3,
        scalars=True,
    )(ocean, tracers, bottom.T, stoich)
    later, sooner = far_pairs(bands, tiles)

    grid = ("ty", "tx")
    first_a = lax.ppermute(first, grid, later)
    rest_a = lax.ppermute(rest, grid, later)
    first_b = lax.ppermute(first, grid, sooner)
    rest_b = lax.ppermute(rest, grid, sooner)
    chip = lax.ppermute(packed, "tx", swaps(tiles, 0))
    up, down, first = kernel(
        row_kernel, [arr(n, *TILE) for n in (WET + 1 + PAIRS, WET + 1 + PAIRS, PAIRS)], 4
    )(*near(packed, chip, first_a, first_b))
    is_odd = odd("comp")
    to = lax.ppermute(jnp.where(is_odd, down, up), axes, swaps(count, 1, place))
    te = lax.ppermute(jnp.where(is_odd, up, down), axes, swaps(count, 0, place))
    state = kernel(
        own_kernel,
        [
            arr(FIELDS + 1, 4, *TILE),
            arr(NTR, 4, *TILE),
            arr(NTR, 2, *TILE),
            arr(2 * len(AUX), *TILE),
        ],
        8,
        [(FIELDS + 1,), (6,), (4,), (4,)],
    )(*near(packed, chip, first, rest_a, rest_b, te, to, yields))
    raw, part, q1_own, aux = near(*state)
    rows, *rest = kernel(
        edge_kernel,
        [arr(comps, 3, ROWS, 256), arr(NTR, 4, *TILE)] + [arr(n, *TILE) for n in (4, 4, 2)],
        6,
        [(4,), (4,), (8,)],
    )(raw, part, aux, *near(te, to, yields))
    gathered = lax.all_to_all(rows, "comp", 0, 0, tiled=True)
    (tracers_out,) = kernel(
        last_kernel, [jax.ShapeDtypeStruct((NTR, 1, ROWS, 256), jnp.float32)], 7, [(4,)]
    )(q1_own, aux, *near(*rest, yields))
    return jnp.swapaxes(gathered, 0, 1).reshape(3, comps * ROWS, 256), tracers_out


def solution(mesh):
    in_specs = (P(None, "ty", "tx"), P(None, "ty", "comp", "tx"), P("ty", "tx"), P())
    out_specs = (P(None, "ty", "tx"), P(None, "ty", "comp", "tx"))
    return jax.shard_map(shards, mesh=mesh, in_specs=in_specs, out_specs=out_specs, check_vma=False)
```

```python
import jax
import jax.numpy as jnp
from jax import lax
from jax.experimental import pallas as pl
from jax.experimental.pallas import tpu as pltpu
from jax.sharding import PartitionSpec as P


LEV = 64
NTR = 19
ROWS = 8
FIELDS = 22
U, V, T, WET = 19, 20, 21, 22
PAIRS = 12
AUX = (
    "w_s", "p_e", "p_h", "sun_e", "sun_h", "heat_e", "heat_h", "cols_e", "rows_h", "u1_s",
    "u1_e", "v1_s", "v1_h", "t1_s", "sun2", "heat2",
)
VMEM = pltpu.VMEM
TILE = (ROWS, 128)


def lanes():
    return lax.broadcasted_iota(jnp.int32, TILE, 1)


def subs():
    return lax.broadcasted_iota(jnp.int32, TILE, 0)


def half_turn(x):
    return pltpu.roll(x, LEV, 1)


def mix(a, b):
    return jnp.where(lanes() < LEV, a, b)


def own_of(w):
    return [mix(w[4], w[0]), mix(w[5], w[1])]


def edge_of(w):
    return [w[2], w[3]]


def each(f, *lists):
    return [f(*args) for args in zip(*lists)]


def next_col(x):
    return x[1:] + [half_turn(x[0])]


def prev_col(x):
    return [half_turn(x[-1])] + x[:-1]


def next_split(s, e):
    return [s[1], mix(half_turn(s[0]), e[0])], [e[1], s[0]]


def prev_split(s, e):
    return [mix(e[1], half_turn(s[1])), s[0]], [s[1], e[0]]


def next_row(o, h):
    edge = subs() == 0
    return (
        [pltpu.roll(jnp.where(edge, b, a), ROWS - 1, 0) for a, b in zip(o, h)],
        [pltpu.roll(jnp.where(edge, a, b), ROWS - 1, 0) for a, b in zip(o, h)],
    )


def prev_row(o, h):
    edge = subs() == ROWS - 1
    return (
        [pltpu.roll(jnp.where(edge, b, a), 1, 0) for a, b in zip(o, h)],
        [pltpu.roll(jnp.where(edge, a, b), 1, 0) for a, b in zip(o, h)],
    )


def minmod(a, b):
    return jnp.maximum(jnp.minimum(a, b), jnp.minimum(jnp.maximum(a, b), 0.0))


def upwind(fac, left, right):
    return fac * jnp.where(fac > 0.0, left, right)


def minus(x, y):
    return each(lambda a, b: a - b, x, y)


def col_divergence(q, fac):
    d = minus(next_col(q), q)
    m = each(minmod, d, prev_col(d))
    left = each(lambda a, b: (a + a) + b, q, m)
    right = each(lambda a, b: (a + a) - b, q, m)
    flux = each(upwind, fac, left, next_col(right))
    return minus(flux, prev_col(flux))


def split_divergence(s, e, fac_s, fac_e):
    n_s, n_e = next_split(s, e)
    d_s, d_e = minus(n_s, s), minus(n_e, e)
    b_s, b_e = prev_split(d_s, d_e)
    m_s, m_e = each(minmod, d_s, b_s), each(minmod, d_e, b_e)
    r_s = each(lambda a, b: (a + a) - b, s, m_s)
    r_e = each(lambda a, b: (a + a) - b, e, m_e)
    n_s, n_e = next_split(r_s, r_e)
    f_s = each(lambda f, a, b, c: upwind(f, (a + a) + b, c), fac_s, s, m_s, n_s)
    f_e = each(lambda f, a, b, c: upwind(f, (a + a) + b, c), fac_e, e, m_e, n_e)
    return minus(f_s, prev_split(f_s, f_e)[0])


def row_divergence(o, h, fac_o, fac_h):
    n_o, n_h = next_row(o, h)
    d_o, d_h = minus(n_o, o), minus(n_h, h)
    b_o, b_h = prev_row(d_o, d_h)
    m_o, m_h = each(minmod, d_o, b_o), each(minmod, d_h, b_h)
    r_o = each(lambda a, b: (a + a) - b, o, m_o)
    r_h = each(lambda a, b: (a + a) - b, h, m_h)
    n_o, n_h = next_row(r_o, r_h)
    f_o = each(lambda f, a, b, c: upwind(f, (a + a) + b, c), fac_o, o, m_o, n_o)
    f_h = each(lambda f, a, b, c: upwind(f, (a + a) + b, c), fac_h, h, m_h, n_h)
    p_o, p_h = prev_row(f_o, f_h)
    return minus(f_o, p_o), minus(f_h, p_h)


def half_factor(vel, wet, next_vel, next_wet):
    return 0.5 * (0.08 * (0.5 * (vel + next_vel) * wet * next_wet))


def col_factor(vel, wet):
    return each(half_factor, vel, wet, next_col(vel), next_col(wet))


def split_factor(vel_s, vel_e, wet_s, wet_e):
    n_s, n_e = next_split(vel_s, vel_e)
    w_s, w_e = next_split(wet_s, wet_e)
    return each(half_factor, vel_s, wet_s, n_s, w_s), each(half_factor, vel_e, wet_e, n_e, w_e)


def row_factor(vel_o, vel_h, wet_o, wet_h):
    n_o, n_h = next_row(vel_o, vel_h)
    w_o, w_h = next_row(wet_o, wet_h)
    return each(half_factor, vel_o, wet_o, n_o, w_o), each(half_factor, vel_h, wet_h, n_h, w_h)


def level_sum(tiles, inclusive):
    r = lax.rem(lax.broadcasted_iota(jnp.int32, (256, 128), 0), 128)
    c = lax.broadcasted_iota(jnp.int32, (256, 128), 1)
    above = (r <= c) if inclusive else (r < c)
    ladder = jnp.where(((r < LEV) == (c < LEV)) & above, 1.0, 0.0).astype(jnp.bfloat16)
    x = jnp.concatenate(tiles, axis=0)
    major = x.astype(jnp.bfloat16)
    minor = (x - major.astype(jnp.float32)).astype(jnp.bfloat16)
    out = jnp.dot(
        jnp.concatenate([major, minor], axis=1), ladder, preferred_element_type=jnp.float32
    )
    return [out[ROWS * i : ROWS * (i + 1)] for i in range(len(tiles))]


def optics(chloro, wet):
    absorb = each(lambda a, w: (0.04 + 0.03 * jnp.maximum(a, 0.0)) * w, chloro, wet)
    sun = [jnp.exp(-s) for s in level_sum(absorb, False)]
    heat = each(lambda s, a, w: s * (1.0 - jnp.exp(-a)) * w, sun, absorb, wet)
    return sun, heat


def east_speed(u, v, n, b, w):
    return each(
        lambda u, v, n, b, w: w * (0.95 * u + 0.2 * (v - 0.5 * (n - b))), u, v, n, b, w
    )


def north_speed(u, v, n, b, w):
    return each(
        lambda u, v, n, b, w: w * (0.95 * v - 0.2 * (u + 0.5 * (n - b))), u, v, n, b, w
    )


def plus(x, y):
    return each(lambda a, b: a + b, x, y)


def warmed(t, heat, rows, cols, w):
    return each(
        lambda t, heat, r, c, w: w * (t + 0.2 * (2.0 * heat + 0.2 * (r + c - 4.0 * t))),
        t, heat, rows, cols, w,
    )


def reaction(adv, sun, temp):
    n, p, c, z, d = [jnp.maximum(a, 0.0) for a in adv]
    uptake = sun / (sun + 0.2) * n / (n + 0.5) * jnp.exp(0.1 * temp)
    growth = uptake * p
    grazing = 0.8 * z * p * p / (p * p + 0.3)
    dying = 0.1 * p
    remin = 0.2 * d
    core = [
        remin - growth,
        growth - grazing - dying,
        0.3 * (0.5 * p - c) + 0.2 * growth,
        0.3 * grazing - 0.05 * z,
        dying + 0.7 * grazing + 0.05 * z - remin,
    ]
    return core, 0.2 * (growth - remin)


def odd(name):
    return lax.rem(lax.axis_index(name), 2) == 1


def wet_tiles(depth):
    level = lax.rem(lanes(), LEV).astype(jnp.float32)
    return [
        jnp.where(level < mix(depth[:, c : c + 1], depth[:, c + 1 : c + 2]), 1.0, 0.0)
        for c in (0, 2)
    ]


def middle():
    return (subs() >= 2) & (subs() < 6)


def pack_kernel(
    ocean_ref, tr_ref, bot_ref, stoich_ref, out_ref, first_ref, rest_ref, yield_ref
):
    for j in range(NTR - 5):
        yield_ref[j] = jnp.full(TILE, stoich_ref[j], jnp.float32)
    start = pl.multiple_of(lax.axis_index("comp") * ROWS, ROWS)
    rows = pl.ds(start, ROWS)
    band = bot_ref.shape[1]
    row = lax.broadcasted_iota(jnp.int32, (ROWS, band), 0) + start
    pick = row == lax.broadcasted_iota(jnp.int32, (ROWS, band), 1)
    depth = jnp.zeros(TILE, jnp.float32)
    for c in range(4):
        line = bot_ref[c : c + 1, :].astype(jnp.float32)
        depth = jnp.where(
            lanes() == c, jnp.sum(jnp.where(pick, line, 0.0), axis=1, keepdims=True), depth
        )
    out_ref[2 * FIELDS] = depth
    rest_ref[PAIRS + FIELDS] = depth
    flip = odd("tx")
    wet = wet_tiles(depth)

    def near_tile(f):
        if f < 0:
            return jnp.zeros(TILE, jnp.float32)
        if f == WET:
            return jnp.where(flip, wet[1], wet[0])
        x = tr_ref[f, 0] if f < NTR else ocean_ref[f - NTR, rows, :]
        a, b = x[:, :128], x[:, 128:]
        out_ref[2 * f] = a
        out_ref[2 * f + 1] = b
        rest_ref[PAIRS + f] = jnp.where(flip, a, b)
        return jnp.where(flip, b, a)

    for k in range(PAIRS):
        x, y = near_tile(2 * k - 1), pltpu.roll(near_tile(2 * k), 4, 0)
        first_ref[k] = jnp.where(middle(), y, x)
        rest_ref[k] = jnp.where(middle(), x, y)


def row_kernel(own_ref, chip_ref, ca_ref, cb_ref, up_ref, down_ref, first_ref):
    flip = odd("tx")
    sub = subs()
    upper = sub < 4

    def strip(f, a, b):
        a, b = mix(a, half_turn(b)), pltpu.roll(mix(half_turn(a), b), 4, 0)
        up_ref[f] = jnp.where(upper, a, b)
        down_ref[f] = jnp.where(upper, b, a)

    for f in range(FIELDS):
        strip(f, own_ref[2 * f], own_ref[2 * f + 1])
    strip(WET, *wet_tiles(own_ref[2 * FIELDS]))
    wet = wet_tiles(chip_ref[2 * FIELDS])

    def edge(f, far):
        if f < 0:
            return [far, far]
        west, east = wet if f == WET else (chip_ref[2 * f], chip_ref[2 * f + 1])
        w = jnp.where(flip, east, far)
        e = jnp.where(flip, far, west)
        return [mix(w, half_turn(e)), mix(half_turn(w), e)]

    for k in range(PAIRS):
        far = ca_ref[k] + cb_ref[k]
        first_ref[k] = far
        a, b, c, d = edge(2 * k - 1, far) + edge(2 * k, pltpu.roll(far, 4, 0))
        turned = pltpu.roll(c, 4, 0)
        up_ref[WET + 1 + k] = jnp.where(
            upper,
            jnp.where(sub < 2, a, pltpu.roll(b, 2, 0)),
            jnp.where(sub < 6, turned, pltpu.roll(d, 6, 0)),
        )
        down_ref[WET + 1 + k] = jnp.where(
            upper,
            jnp.where(sub < 2, pltpu.roll(d, 2, 0), turned),
            jnp.where(sub < 6, pltpu.roll(b, 6, 0), a),
        )


def save(ref, tiles):
    for i, x in enumerate(tiles):
        ref[i] = x


def load(ref, *names):
    if not names:
        return [ref[i] for i in range(ref.shape[0])]
    return [[ref[2 * AUX.index(n)], ref[2 * AUX.index(n) + 1]] for n in names]


def own_kernel(
    own_ref, chip_ref, first_ref, ra_ref, rb_ref, te_ref, to_ref, stoich_ref, raw_ref, part_ref,
    q1_ref, aux_ref, near_ref, fc_ref, fr_ref, g_ref,
):
    flip = odd("tx")
    even = jnp.logical_not(odd("comp"))
    mid = middle()
    for k in range(PAIRS):
        c, r = first_ref[k], ra_ref[k] + rb_ref[k]
        if k:
            near_ref[2 * k - 1] = jnp.where(mid, r, c)
        near_ref[2 * k] = pltpu.roll(jnp.where(mid, c, r), 4, 0)

    def arrange(a, b):
        pairs = ((a[0], b[1]), (b[0], a[2]), (a[1], b[2]))
        out = []
        for low, high in pairs:
            out += [mix(low, half_turn(high)), mix(half_turn(low), high)]
        return out

    def blocks(f):
        n, d = near_ref[f], ra_ref[PAIRS + f] + rb_ref[PAIRS + f]
        c0, c1 = chip_ref[2 * f], chip_ref[2 * f + 1]
        west = jnp.where(flip, c0, d), jnp.where(flip, c1, n)
        east = jnp.where(flip, n, c0), jnp.where(flip, d, c1)
        return west, (own_ref[2 * f], own_ref[2 * f + 1]), east

    def wide(f):
        return arrange(*zip(*blocks(f)))

    def halo(f):
        first = (subs() < 4) == even
        te, to = te_ref[f], to_ref[f]
        return [jnp.where(first, te, to), pltpu.roll(jnp.where(first, to, te), 4, 0)]

    u_w, v_w, t_w = [wide(f) for f in (U, V, T)]
    far = wet_tiles(ra_ref[PAIRS + FIELDS] + rb_ref[PAIRS + FIELDS])
    close = wet_tiles(chip_ref[2 * FIELDS])
    own = wet_tiles(own_ref[2 * FIELDS])
    west = [jnp.where(flip, c, d) for c, d in zip(close, far)]
    east = [jnp.where(flip, d, c) for c, d in zip(close, far)]
    w_w = arrange(*zip(west, own, east))
    u_h, v_h, t_h, w_h = [halo(f) for f in (U, V, T, WET)]
    u_s, v_s, t_s, w_s = [own_of(x) for x in (u_w, v_w, t_w, w_w)]
    w_e = edge_of(w_w)
    for f, wd, h in ((U, u_w, u_h), (V, v_w, v_h), (T, t_w, t_h), (WET, w_w, w_h)):
        save(raw_ref.at[f], edge_of(wd) + h)

    press = [0.05 * s for s in level_sum(t_w + t_h, True)]
    p_w, p_h = press[:6], press[6:]
    p_s = own_of(p_w)
    q_w, q_h = wide(2), halo(2)
    sun, heat = optics(own_of(q_w) + edge_of(q_w) + q_h, w_s + w_e + w_h)
    u1_w = east_speed(u_w, v_w, next_col(p_w), prev_col(p_w), w_w)
    (n_s, n_h), (b_s, b_h) = next_row(p_s, p_h), prev_row(p_s, p_h)
    v1_s = north_speed(u_s, v_s, n_s, b_s, w_s)
    v1_h = north_speed(u_h, v_h, n_h, b_h, w_h)
    (n_s, n_h), (b_s, b_h) = next_row(t_s, t_h), prev_row(t_s, t_h)
    around = plus(next_col(t_w), prev_col(t_w))
    t1_s = warmed(t_s, heat[:2], plus(n_s, b_s), own_of(around), w_s)
    save(fc_ref, col_factor(u1_w, w_w))
    fr_s, fr_h = row_factor(v1_s, v1_h, w_s, w_h)
    save(fr_ref, fr_s + fr_h)

    def advect(f):
        q_w, q_h = wide(f), halo(f)
        q_s, q_e = own_of(q_w), edge_of(q_w)
        col = col_divergence(q_w, load(fc_ref))
        fr = load(fr_ref)
        r_s, r_h = row_divergence(q_s, q_h, fr[:2], fr[2:])
        save(raw_ref.at[f], q_e + q_h)
        save(part_ref.at[f], minus(q_e, edge_of(col)) + minus(q_h, r_h))
        return minus(minus(q_s, own_of(col)), r_s)

    first = [advect(f) for f in range(5)]
    gain, chloro = [], []
    for i in range(2):
        core, g = reaction([first[f][i] for f in range(5)], sun[i], t1_s[i])
        gain.append(g)
        for f in range(5):
            q1_ref[f, i] = (first[f][i] + 0.2 * core[f]) * w_s[i]
        chloro.append((first[2][i] + 0.2 * core[2]) * w_s[i])
    sun2, heat2 = optics(chloro, w_s)
    save(g_ref, gain + w_s)
    values = dict(
        w_s=w_s, p_e=edge_of(p_w), p_h=p_h, sun_e=sun[2:4], sun_h=sun[4:], heat_e=heat[2:4],
        heat_h=heat[4:], cols_e=edge_of(around), rows_h=plus(n_h, b_h), u1_s=own_of(u1_w),
        u1_e=edge_of(u1_w), v1_s=v1_s, v1_h=v1_h, t1_s=t1_s, sun2=sun2, heat2=heat2,
    )
    save(aux_ref, [x for n in AUX for x in values[n]])

    def others(f, _):
        s = stoich_ref[f - 5]
        k = load(g_ref)
        out = each(lambda a, g, w: (a + s * g) * w, advect(f), k[:2], k[2:])
        save(q1_ref.at[f], out)
        return 0

    lax.fori_loop(5, NTR, others, 0, unroll=2)


def plain(x):
    return [mix(x[0], half_turn(x[1])), mix(half_turn(x[0]), x[1])]


def corners(te_ref, to_ref, k):
    sub4 = subs() < 4
    swapped = odd("comp")
    te, to = te_ref[WET + 1 + k], to_ref[WET + 1 + k]
    b, a = jnp.where(swapped, to, te), jnp.where(swapped, te, to)
    return (
        [jnp.where(sub4, b, a), jnp.where(sub4, pltpu.roll(b, 6, 0), pltpu.roll(a, 2, 0))],
        [
            pltpu.roll(jnp.where(sub4, a, b), 4, 0),
            jnp.where(sub4, pltpu.roll(b, 2, 0), pltpu.roll(a, 6, 0)),
        ],
    )


def halves(ref, f):
    x = load(ref.at[f])
    return x[:2], x[2:]


def ocean_kernel(
    raw_ref, aux_ref, te_ref, to_ref, ocean_ref, fc_ref, fr_ref, t1_ref, c2_ref, r2_ref, t2_ref
):
    (u_c, v_c), (t_c, w_c) = corners(te_ref, to_ref, (U + 1) // 2), corners(te_ref, to_ref, (T + 1) // 2)
    (u_e, u_h), (v_e, v_h), (t_e, t_h), (w_e, w_h) = [halves(raw_ref, f) for f in (U, V, T, WET)]
    w_s, p_e, p_h = load(aux_ref, "w_s", "p_e", "p_h")
    p_c = [0.05 * s for s in level_sum(t_c, True)]

    (n_h, n_c), (b_h, b_c) = next_split(p_h, p_c), prev_split(p_h, p_c)
    u1_h = east_speed(u_h, v_h, n_h, b_h, w_h)
    u1_c = east_speed(u_c, v_c, n_c, b_c, w_c)
    (n_e, n_c), (b_e, b_c) = next_row(p_e, p_c), prev_row(p_e, p_c)
    v1_e = north_speed(u_e, v_e, n_e, b_e, w_e)
    v1_c = north_speed(u_c, v_c, n_c, b_c, w_c)
    heat_e, heat_h, cols_e, rows_h = load(aux_ref, "heat_e", "heat_h", "cols_e", "rows_h")
    rows_e = plus(next_row(t_e, t_c)[0], prev_row(t_e, t_c)[0])
    t1_e = warmed(t_e, heat_e, rows_e, cols_e, w_e)
    cols_h = plus(next_split(t_h, t_c)[0], prev_split(t_h, t_c)[0])
    t1_h = warmed(t_h, heat_h, rows_h, cols_h, w_h)
    fc_h, fc_c = split_factor(u1_h, u1_c, w_h, w_c)
    save(fc_ref, fc_h + fc_c)
    fr_e, fr_c = row_factor(v1_e, v1_c, w_e, w_c)
    save(fr_ref, fr_e + fr_c)

    u1_s, u1_e, v1_s, v1_h, t1_s, _, heat2 = load(
        aux_ref, "u1_s", "u1_e", "v1_s", "v1_h", "t1_s", "sun2", "heat2"
    )
    p1 = [0.05 * s for s in level_sum(t1_s + t1_e + t1_h, True)]
    p_s, p_e, p_h = p1[:2], p1[2:4], p1[4:]
    (n_s, n_e), (b_s, b_e) = next_split(p_s, p_e), prev_split(p_s, p_e)
    u2_s = east_speed(u1_s, v1_s, n_s, b_s, w_s)
    u2_e = east_speed(u1_e, v1_e, n_e, b_e, w_e)
    (n_s, n_h), (b_s, b_h) = next_row(p_s, p_h), prev_row(p_s, p_h)
    v2_s = north_speed(u1_s, v1_s, n_s, b_s, w_s)
    v2_h = north_speed(u1_h, v1_h, n_h, b_h, w_h)
    rows = plus(next_row(t1_s, t1_h)[0], prev_row(t1_s, t1_h)[0])
    cols = plus(next_split(t1_s, t1_e)[0], prev_split(t1_s, t1_e)[0])
    t2 = warmed(t1_s, heat2, rows, cols, w_s)

    save(t1_ref, t1_e + t1_h)
    save(t2_ref, t2)
    for k, x in enumerate((u2_s, v2_s, t2)):
        for i, tile in enumerate(plain(x)):
            for peer in range(ocean_ref.shape[0]):
                ocean_ref[peer, k, :, 128 * i : 128 * (i + 1)] = tile

    fc_s, fc_e = split_factor(u2_s, u2_e, w_s, w_e)
    save(c2_ref, fc_s + fc_e)
    fr_s, fr_h = row_factor(v2_s, v2_h, w_s, w_h)
    save(r2_ref, fr_s + fr_h)


def last_kernel(
    raw_ref, part_ref, aux_ref, te_ref, to_ref, stoich_ref, fc_ref, fr_ref, t1_ref, q1_ref,
    c2_ref, r2_ref, t2_ref, out_ref, q_ref, g_ref, g2_ref,
):
    def advect1(f, q_c):
        q_e, q_h = halves(raw_ref, f)
        fc, fr = load(fc_ref), load(fr_ref)
        row = row_divergence(q_e, q_c, fr[:2], fr[2:])[0]
        col = split_divergence(q_h, q_c, fc[:2], fc[2:])
        return minus(load(part_ref.at[f]), row + col)

    c = [corners(te_ref, to_ref, k) for k in range(3)]
    core_corners = [c[0][1], c[1][0], c[1][1], c[2][0], c[2][1]]
    first = [advect1(f, core_corners[f]) for f in range(5)]
    sun_e, sun_h = load(aux_ref, "sun_e", "sun_h")
    w_e, w_h = halves(raw_ref, WET)
    w_four, sun, t1_four, gain = w_e + w_h, sun_e + sun_h, load(t1_ref), []
    for i in range(4):
        core, g = reaction([first[f][i] for f in range(5)], sun[i], t1_four[i])
        gain.append(g)
        for f in range(5):
            q_ref[f, i] = (first[f][i] + 0.2 * core[f]) * w_four[i]
    save(g_ref, gain + w_four)

    def others1(k, _):
        both = corners(te_ref, to_ref, k)
        for j in range(2):
            f = 2 * k - 1 + j
            s = stoich_ref[f - 5]
            g = load(g_ref)
            out = each(lambda a, g, w: (a + s * g) * w, advect1(f, both[j]), g[:4], g[4:])
            save(q_ref.at[f], out)
        return 0

    lax.fori_loop(3, 10, others1, 0)

    w_s, sun2 = load(aux_ref, "w_s", "sun2")
    t2 = load(t2_ref)

    def advect2(f):
        q_s, x = load(q1_ref.at[f]), load(q_ref.at[f])
        fc, fr = load(c2_ref), load(r2_ref)
        row = row_divergence(q_s, x[2:], fr[:2], fr[2:])[0]
        return minus(minus(q_s, split_divergence(q_s, x[:2], fc[:2], fc[2:])), row)

    def finish(f, tiles):
        for i, x in enumerate(plain(tiles)):
            out_ref[f, 0, :, 128 * i : 128 * (i + 1)] = x

    first = [advect2(f) for f in range(5)]
    done = [[] for _ in range(5)]
    gain = []
    for i in range(2):
        core, g = reaction([first[f][i] for f in range(5)], sun2[i], t2[i])
        gain.append(g)
        for f in range(5):
            done[f].append((first[f][i] + 0.2 * core[f]) * w_s[i])
    for f in range(5):
        finish(f, done[f])
    save(g2_ref, gain + w_s)

    def others2(f, _):
        s = stoich_ref[f - 5]
        k = load(g2_ref)
        finish(f, each(lambda a, g, w: (a + s * g) * w, advect2(f), k[:2], k[2:]))
        return 0

    lax.fori_loop(5, NTR, others2, 0, unroll=2)


def swaps(count, first, place=lambda i: i):
    pairs = []
    for a in range(first, count - 1, 2):
        pairs += [(place(a), place(a + 1)), (place(a + 1), place(a))]
    return pairs


def far_pairs(bands, tiles):
    later, sooner = [], []
    for ty in range(bands):
        for a in range(1, tiles - 1, 2):
            pair = (ty * tiles + a, ty * tiles + a + 1)
            part = 4 * (a + 1) // tiles
            if part == 1 or (part == 2 and 4 * ty < 3 * bands):
                pair = pair[::-1]
            later.append(pair)
            sooner.append(pair[::-1])
    return later, sooner


def shards(ocean, tracers, bottom, stoich):
    comps = lax.axis_size("comp")
    bands = lax.axis_size("ty")
    tiles = lax.axis_size("tx")
    vmem = pl.BlockSpec(memory_space=VMEM)

    def arr(*dims):
        return VMEM(dims, jnp.float32)

    def near(*args):
        return [pltpu.with_memory_space_constraint(a, VMEM) for a in args]

    def place(row):
        return (row % comps) * bands + row // comps

    axes = ("comp", "ty")
    count = comps * bands

    def kernel(body, outs, ins, scratch=(), scalars=False):
        return pl.pallas_call(
            body,
            out_shape=tuple(outs),
            in_specs=[vmem] * ins + [pl.BlockSpec(memory_space=pltpu.SMEM)] * scalars,
            out_specs=(vmem,) * len(outs),
            scratch_shapes=[VMEM((*n, *TILE), jnp.float32) for n in scratch],
        )

    packed, first, rest, yields = kernel(
        pack_kernel,
        [arr(n, *TILE) for n in (2 * FIELDS + 1, PAIRS, PAIRS + FIELDS + 1, NTR - 5)],
        3,
        scalars=True,
    )(ocean, tracers, bottom.T, stoich)
    later, sooner = far_pairs(bands, tiles)

    grid = ("ty", "tx")
    first_a = lax.ppermute(first, grid, later)
    rest_a = lax.ppermute(rest, grid, later)
    first_b = lax.ppermute(first, grid, sooner)
    rest_b = lax.ppermute(rest, grid, sooner)
    chip = lax.ppermute(packed, "tx", swaps(tiles, 0))
    up, down, first = kernel(
        row_kernel, [arr(n, *TILE) for n in (WET + 1 + PAIRS, WET + 1 + PAIRS, PAIRS)], 4
    )(*near(packed, chip, first_a, first_b))
    is_odd = odd("comp")
    to = lax.ppermute(jnp.where(is_odd, down, up), axes, swaps(count, 1, place))
    te = lax.ppermute(jnp.where(is_odd, up, down), axes, swaps(count, 0, place))
    state = kernel(
        own_kernel,
        [
            arr(FIELDS + 1, 4, *TILE),
            arr(NTR, 4, *TILE),
            arr(NTR, 2, *TILE),
            arr(2 * len(AUX), *TILE),
        ],
        8,
        [(FIELDS + 1,), (6,), (4,), (4,)],
    )(*near(packed, chip, first, rest_a, rest_b, te, to, yields))
    raw, part, q1_own, aux = near(*state)
    rows, fc, fr, t1, c2, r2, t2 = kernel(
        ocean_kernel,
        [arr(comps, 3, ROWS, 256)] + [arr(n, *TILE) for n in (4, 4, 4, 4, 4, 2)],
        4,
    )(raw, aux, *near(te, to))
    gathered = lax.all_to_all(rows, "comp", 0, 0, tiled=True)
    (tracers_out,) = kernel(
        last_kernel,
        [jax.ShapeDtypeStruct((NTR, 1, ROWS, 256), jnp.float32)],
        13,
        [(NTR, 4), (8,), (4,)],
    )(raw, part, aux, *near(te, to, yields, fc, fr, t1), q1_own, *near(c2, r2, t2))
    return jnp.swapaxes(gathered, 0, 1).reshape(3, comps * ROWS, 256), tracers_out


def solution(mesh):
    in_specs = (P(None, "ty", "tx"), P(None, "ty", "comp", "tx"), P("ty", "tx"), P())
    out_specs = (P(None, "ty", "tx"), P(None, "ty", "comp", "tx"))
    return jax.shard_map(shards, mesh=mesh, in_specs=in_specs, out_specs=out_specs, check_vma=False)
```

```python
import jax
import jax.numpy as jnp
from jax import lax
from jax.experimental import pallas as pl
from jax.experimental.pallas import tpu as pltpu
from jax.sharding import PartitionSpec as P


LEV = 64
NTR = 19
ROWS = 8
FIELDS = 22
U, V, T, WET = 19, 20, 21, 22
PAIRS = 12
AUX = (
    "w_s", "p_e", "p_h", "sun_e", "sun_h", "heat_e", "heat_h", "cols_e", "rows_h", "u1_s",
    "u1_e", "v1_s", "v1_h", "t1_s", "sun2", "heat2",
)
VMEM = pltpu.VMEM
TILE = (ROWS, 128)


def lanes():
    return lax.broadcasted_iota(jnp.int32, TILE, 1)


def subs():
    return lax.broadcasted_iota(jnp.int32, TILE, 0)


def half_turn(x):
    return pltpu.roll(x, LEV, 1)


def mix(a, b):
    return jnp.where(lanes() < LEV, a, b)


def own_of(w):
    return [mix(w[4], w[0]), mix(w[5], w[1])]


def edge_of(w):
    return [w[2], w[3]]


def each(f, *lists):
    return [f(*args) for args in zip(*lists)]


def next_col(x):
    return x[1:] + [half_turn(x[0])]


def prev_col(x):
    return [half_turn(x[-1])] + x[:-1]


def next_split(s, e):
    return [s[1], mix(half_turn(s[0]), e[0])], [e[1], s[0]]


def prev_split(s, e):
    return [mix(e[1], half_turn(s[1])), s[0]], [s[1], e[0]]


def next_row(o, h):
    edge = subs() == 0
    return (
        [pltpu.roll(jnp.where(edge, b, a), ROWS - 1, 0) for a, b in zip(o, h)],
        [pltpu.roll(jnp.where(edge, a, b), ROWS - 1, 0) for a, b in zip(o, h)],
    )


def prev_row(o, h):
    edge = subs() == ROWS - 1
    return (
        [pltpu.roll(jnp.where(edge, b, a), 1, 0) for a, b in zip(o, h)],
        [pltpu.roll(jnp.where(edge, a, b), 1, 0) for a, b in zip(o, h)],
    )


def minmod(a, b):
    return jnp.maximum(jnp.minimum(a, b), jnp.minimum(jnp.maximum(a, b), 0.0))


def upwind(fac, left, right):
    return fac * jnp.where(fac > 0.0, left, right)


def minus(x, y):
    return each(lambda a, b: a - b, x, y)


def col_divergence(q, fac):
    d = minus(next_col(q), q)
    m = each(minmod, d, prev_col(d))
    left = each(lambda a, b: (a + a) + b, q, m)
    right = each(lambda a, b: (a + a) - b, q, m)
    flux = each(upwind, fac, left, next_col(right))
    return minus(flux, prev_col(flux))


def split_divergence(s, e, fac_s, fac_e):
    n_s, n_e = next_split(s, e)
    d_s, d_e = minus(n_s, s), minus(n_e, e)
    b_s, b_e = prev_split(d_s, d_e)
    m_s, m_e = each(minmod, d_s, b_s), each(minmod, d_e, b_e)
    r_s = each(lambda a, b: (a + a) - b, s, m_s)
    r_e = each(lambda a, b: (a + a) - b, e, m_e)
    n_s, n_e = next_split(r_s, r_e)
    f_s = each(lambda f, a, b, c: upwind(f, (a + a) + b, c), fac_s, s, m_s, n_s)
    f_e = each(lambda f, a, b, c: upwind(f, (a + a) + b, c), fac_e, e, m_e, n_e)
    return minus(f_s, prev_split(f_s, f_e)[0])


def row_divergence(o, h, fac_o, fac_h):
    n_o, n_h = next_row(o, h)
    d_o, d_h = minus(n_o, o), minus(n_h, h)
    b_o, b_h = prev_row(d_o, d_h)
    m_o, m_h = each(minmod, d_o, b_o), each(minmod, d_h, b_h)
    r_o = each(lambda a, b: (a + a) - b, o, m_o)
    r_h = each(lambda a, b: (a + a) - b, h, m_h)
    n_o, n_h = next_row(r_o, r_h)
    f_o = each(lambda f, a, b, c: upwind(f, (a + a) + b, c), fac_o, o, m_o, n_o)
    f_h = each(lambda f, a, b, c: upwind(f, (a + a) + b, c), fac_h, h, m_h, n_h)
    p_o, p_h = prev_row(f_o, f_h)
    return minus(f_o, p_o), minus(f_h, p_h)


def half_factor(vel, wet, next_vel, next_wet):
    return 0.5 * (0.08 * (0.5 * (vel + next_vel) * wet * next_wet))


def col_factor(vel, wet):
    return each(half_factor, vel, wet, next_col(vel), next_col(wet))


def split_factor(vel_s, vel_e, wet_s, wet_e):
    n_s, n_e = next_split(vel_s, vel_e)
    w_s, w_e = next_split(wet_s, wet_e)
    return each(half_factor, vel_s, wet_s, n_s, w_s), each(half_factor, vel_e, wet_e, n_e, w_e)


def row_factor(vel_o, vel_h, wet_o, wet_h):
    n_o, n_h = next_row(vel_o, vel_h)
    w_o, w_h = next_row(wet_o, wet_h)
    return each(half_factor, vel_o, wet_o, n_o, w_o), each(half_factor, vel_h, wet_h, n_h, w_h)


def level_sum(tiles, inclusive):
    r = lax.rem(lax.broadcasted_iota(jnp.int32, (256, 128), 0), 128)
    c = lax.broadcasted_iota(jnp.int32, (256, 128), 1)
    above = (r <= c) if inclusive else (r < c)
    ladder = jnp.where(((r < LEV) == (c < LEV)) & above, 1.0, 0.0).astype(jnp.bfloat16)
    x = jnp.concatenate(tiles, axis=0)
    major = x.astype(jnp.bfloat16)
    minor = (x - major.astype(jnp.float32)).astype(jnp.bfloat16)
    out = jnp.dot(
        jnp.concatenate([major, minor], axis=1), ladder, preferred_element_type=jnp.float32
    )
    return [out[ROWS * i : ROWS * (i + 1)] for i in range(len(tiles))]


def optics(chloro, wet):
    absorb = each(lambda a, w: (0.04 + 0.03 * jnp.maximum(a, 0.0)) * w, chloro, wet)
    sun = [jnp.exp(-s) for s in level_sum(absorb, False)]
    heat = each(lambda s, a, w: s * (1.0 - jnp.exp(-a)) * w, sun, absorb, wet)
    return sun, heat


def east_speed(u, v, n, b, w):
    return each(
        lambda u, v, n, b, w: w * (0.95 * u + 0.2 * (v - 0.5 * (n - b))), u, v, n, b, w
    )


def north_speed(u, v, n, b, w):
    return each(
        lambda u, v, n, b, w: w * (0.95 * v - 0.2 * (u + 0.5 * (n - b))), u, v, n, b, w
    )


def plus(x, y):
    return each(lambda a, b: a + b, x, y)


def warmed(t, heat, rows, cols, w):
    return each(
        lambda t, heat, r, c, w: w * (t + 0.2 * (2.0 * heat + 0.2 * (r + c - 4.0 * t))),
        t, heat, rows, cols, w,
    )


def reaction(adv, sun, temp):
    n, p, c, z, d = [jnp.maximum(a, 0.0) for a in adv]
    uptake = sun / (sun + 0.2) * n / (n + 0.5) * jnp.exp(0.1 * temp)
    growth = uptake * p
    grazing = 0.8 * z * p * p / (p * p + 0.3)
    dying = 0.1 * p
    remin = 0.2 * d
    core = [
        remin - growth,
        growth - grazing - dying,
        0.3 * (0.5 * p - c) + 0.2 * growth,
        0.3 * grazing - 0.05 * z,
        dying + 0.7 * grazing + 0.05 * z - remin,
    ]
    return core, 0.2 * (growth - remin)


def odd(name):
    return lax.rem(lax.axis_index(name), 2) == 1


def wet_tiles(depth):
    level = lax.rem(lanes(), LEV).astype(jnp.float32)
    return [
        jnp.where(level < mix(depth[:, c : c + 1], depth[:, c + 1 : c + 2]), 1.0, 0.0)
        for c in (0, 2)
    ]


def middle():
    return (subs() >= 2) & (subs() < 6)


def pack_kernel(
    ocean_ref, tr_ref, bot_ref, stoich_ref, out_ref, first_ref, rest_ref, yield_ref
):
    for j in range(NTR - 5):
        yield_ref[j] = jnp.full(TILE, stoich_ref[j], jnp.float32)
    start = pl.multiple_of(lax.axis_index("comp") * ROWS, ROWS)
    rows = pl.ds(start, ROWS)
    band = bot_ref.shape[1]
    row = lax.broadcasted_iota(jnp.int32, (ROWS, band), 0) + start
    pick = row == lax.broadcasted_iota(jnp.int32, (ROWS, band), 1)
    depth = jnp.zeros(TILE, jnp.float32)
    for c in range(4):
        line = bot_ref[c : c + 1, :].astype(jnp.float32)
        depth = jnp.where(
            lanes() == c, jnp.sum(jnp.where(pick, line, 0.0), axis=1, keepdims=True), depth
        )
    out_ref[2 * FIELDS] = depth
    rest_ref[PAIRS + FIELDS] = depth
    flip = odd("tx")
    wet = wet_tiles(depth)

    def near_tile(f):
        if f < 0:
            return jnp.zeros(TILE, jnp.float32)
        if f == WET:
            return jnp.where(flip, wet[1], wet[0])
        x = tr_ref[f, 0] if f < NTR else ocean_ref[f - NTR, rows, :]
        a, b = x[:, :128], x[:, 128:]
        out_ref[2 * f] = a
        out_ref[2 * f + 1] = b
        rest_ref[PAIRS + f] = jnp.where(flip, a, b)
        return jnp.where(flip, b, a)

    for k in range(PAIRS):
        x, y = near_tile(2 * k - 1), pltpu.roll(near_tile(2 * k), 4, 0)
        first_ref[k] = jnp.where(middle(), y, x)
        rest_ref[k] = jnp.where(middle(), x, y)


def row_kernel(own_ref, chip_ref, ca_ref, cb_ref, up_ref, down_ref, first_ref):
    flip = odd("tx")
    sub = subs()
    upper = sub < 4

    def strip(f, a, b):
        a, b = mix(a, half_turn(b)), pltpu.roll(mix(half_turn(a), b), 4, 0)
        up_ref[f] = jnp.where(upper, a, b)
        down_ref[f] = jnp.where(upper, b, a)

    for f in range(FIELDS):
        strip(f, own_ref[2 * f], own_ref[2 * f + 1])
    strip(WET, *wet_tiles(own_ref[2 * FIELDS]))
    wet = wet_tiles(chip_ref[2 * FIELDS])

    def edge(f, far):
        if f < 0:
            return [far, far]
        west, east = wet if f == WET else (chip_ref[2 * f], chip_ref[2 * f + 1])
        w = jnp.where(flip, east, far)
        e = jnp.where(flip, far, west)
        return [mix(w, half_turn(e)), mix(half_turn(w), e)]

    for k in range(PAIRS):
        far = ca_ref[k] + cb_ref[k]
        first_ref[k] = far
        a, b, c, d = edge(2 * k - 1, far) + edge(2 * k, pltpu.roll(far, 4, 0))
        turned = pltpu.roll(c, 4, 0)
        up_ref[WET + 1 + k] = jnp.where(
            upper,
            jnp.where(sub < 2, a, pltpu.roll(b, 2, 0)),
            jnp.where(sub < 6, turned, pltpu.roll(d, 6, 0)),
        )
        down_ref[WET + 1 + k] = jnp.where(
            upper,
            jnp.where(sub < 2, pltpu.roll(d, 2, 0), turned),
            jnp.where(sub < 6, pltpu.roll(b, 6, 0), a),
        )


def save(ref, tiles):
    for i, x in enumerate(tiles):
        ref[i] = x


def load(ref, *names):
    if not names:
        return [ref[i] for i in range(ref.shape[0])]
    return [[ref[2 * AUX.index(n)], ref[2 * AUX.index(n) + 1]] for n in names]


def cols_kernel(
    own_ref, chip_ref, first_ref, ra_ref, rb_ref, s_ref, e_ref, part_ref, aux_ref, near_ref,
    fc_ref,
):
    flip = odd("tx")
    mid = middle()
    for k in range(PAIRS):
        c, r = first_ref[k], ra_ref[k] + rb_ref[k]
        if k:
            near_ref[2 * k - 1] = jnp.where(mid, r, c)
        near_ref[2 * k] = pltpu.roll(jnp.where(mid, c, r), 4, 0)

    def arrange(a, b):
        pairs = ((a[0], b[1]), (b[0], a[2]), (a[1], b[2]))
        out = []
        for low, high in pairs:
            out += [mix(low, half_turn(high)), mix(half_turn(low), high)]
        return out

    def blocks(f):
        n, d = near_ref[f], ra_ref[PAIRS + f] + rb_ref[PAIRS + f]
        c0, c1 = chip_ref[2 * f], chip_ref[2 * f + 1]
        west = jnp.where(flip, c0, d), jnp.where(flip, c1, n)
        east = jnp.where(flip, n, c0), jnp.where(flip, d, c1)
        return west, (own_ref[2 * f], own_ref[2 * f + 1]), east

    def wide(f):
        return arrange(*zip(*blocks(f)))

    u_w, v_w, t_w = [wide(f) for f in (U, V, T)]
    far = wet_tiles(ra_ref[PAIRS + FIELDS] + rb_ref[PAIRS + FIELDS])
    close = wet_tiles(chip_ref[2 * FIELDS])
    own = wet_tiles(own_ref[2 * FIELDS])
    west = [jnp.where(flip, c, d) for c, d in zip(close, far)]
    east = [jnp.where(flip, d, c) for c, d in zip(close, far)]
    w_w = arrange(*zip(west, own, east))
    for f, x in ((U, u_w), (V, v_w), (T, t_w), (WET, w_w)):
        save(s_ref.at[f], own_of(x))
        save(e_ref.at[f], edge_of(x))
    p_w = [0.05 * s for s in level_sum(t_w, True)]
    u1_w = east_speed(u_w, v_w, next_col(p_w), prev_col(p_w), w_w)
    around = plus(next_col(t_w), prev_col(t_w))
    both = [own_of(x) + edge_of(x) for x in (p_w, u1_w, around)]
    save(aux_ref, both[0] + both[1] + both[2])
    save(fc_ref, col_factor(u1_w, w_w))

    def one(f, _):
        q_w = wide(f)
        q_s, q_e = own_of(q_w), edge_of(q_w)
        col = col_divergence(q_w, load(fc_ref))
        save(s_ref.at[f], q_s)
        save(e_ref.at[f], q_e)
        save(part_ref.at[f], minus(q_s, own_of(col)) + minus(q_e, edge_of(col)))
        return 0

    one(0, 0)
    lax.fori_loop(1, NTR, one, 0, unroll=6)


def own_kernel(
    s_ref, e_ref, cols_ref, caux_ref, te_ref, to_ref, stoich_ref, raw_ref, part_ref, q1_ref,
    aux_ref, fr_ref, g_ref,
):
    even = jnp.logical_not(odd("comp"))

    def halo(f):
        first = (subs() < 4) == even
        te, to = te_ref[f], to_ref[f]
        return [jnp.where(first, te, to), pltpu.roll(jnp.where(first, to, te), 4, 0)]

    u_s, v_s, t_s, w_s = [load(s_ref.at[f]) for f in (U, V, T, WET)]
    u_h, v_h, t_h, w_h = [halo(f) for f in (U, V, T, WET)]
    w_e = load(e_ref.at[WET])
    for f, h in ((U, u_h), (V, v_h), (T, t_h), (WET, w_h)):
        save(raw_ref.at[f], load(e_ref.at[f]) + h)
    c = load(caux_ref)
    p_s, p_e, u1_s, u1_e, cols_s, cols_e = [c[i : i + 2] for i in range(0, 12, 2)]
    p_h = [0.05 * s for s in level_sum(t_h, True)]
    sun, heat = optics(load(s_ref.at[2]) + load(e_ref.at[2]) + halo(2), w_s + w_e + w_h)
    (n_s, n_h), (b_s, b_h) = next_row(p_s, p_h), prev_row(p_s, p_h)
    v1_s = north_speed(u_s, v_s, n_s, b_s, w_s)
    v1_h = north_speed(u_h, v_h, n_h, b_h, w_h)
    (n_s, n_h), (b_s, b_h) = next_row(t_s, t_h), prev_row(t_s, t_h)
    t1_s = warmed(t_s, heat[:2], plus(n_s, b_s), cols_s, w_s)
    fr_s, fr_h = row_factor(v1_s, v1_h, w_s, w_h)
    save(fr_ref, fr_s + fr_h)

    def advect(f):
        q_h, c, fr = halo(f), load(cols_ref.at[f]), load(fr_ref)
        r_s, r_h = row_divergence(load(s_ref.at[f]), q_h, fr[:2], fr[2:])
        save(raw_ref.at[f], load(e_ref.at[f]) + q_h)
        save(part_ref.at[f], c[2:] + minus(q_h, r_h))
        return minus(c[:2], r_s)

    first = [advect(f) for f in range(5)]
    gain, chloro = [], []
    for i in range(2):
        core, g = reaction([first[f][i] for f in range(5)], sun[i], t1_s[i])
        gain.append(g)
        for f in range(5):
            q1_ref[f, i] = (first[f][i] + 0.2 * core[f]) * w_s[i]
        chloro.append((first[2][i] + 0.2 * core[2]) * w_s[i])
    sun2, heat2 = optics(chloro, w_s)
    save(g_ref, gain + w_s)
    values = dict(
        w_s=w_s, p_e=p_e, p_h=p_h, sun_e=sun[2:4], sun_h=sun[4:], heat_e=heat[2:4],
        heat_h=heat[4:], cols_e=cols_e, rows_h=plus(n_h, b_h), u1_s=u1_s,
        u1_e=u1_e, v1_s=v1_s, v1_h=v1_h, t1_s=t1_s, sun2=sun2, heat2=heat2,
    )
    save(aux_ref, [x for n in AUX for x in values[n]])

    def others(f, _):
        s = stoich_ref[f - 5]
        k = load(g_ref)
        out = each(lambda a, g, w: (a + s * g) * w, advect(f), k[:2], k[2:])
        save(q1_ref.at[f], out)
        return 0

    lax.fori_loop(5, NTR, others, 0, unroll=2)


def plain(x):
    return [mix(x[0], half_turn(x[1])), mix(half_turn(x[0]), x[1])]


def corners(te_ref, to_ref, k):
    sub4 = subs() < 4
    swapped = odd("comp")
    te, to = te_ref[WET + 1 + k], to_ref[WET + 1 + k]
    b, a = jnp.where(swapped, to, te), jnp.where(swapped, te, to)
    return (
        [jnp.where(sub4, b, a), jnp.where(sub4, pltpu.roll(b, 6, 0), pltpu.roll(a, 2, 0))],
        [
            pltpu.roll(jnp.where(sub4, a, b), 4, 0),
            jnp.where(sub4, pltpu.roll(b, 2, 0), pltpu.roll(a, 6, 0)),
        ],
    )


def halves(ref, f):
    x = load(ref.at[f])
    return x[:2], x[2:]


def ocean_kernel(
    raw_ref, aux_ref, te_ref, to_ref, ocean_ref, fc_ref, fr_ref, t1_ref, c2_ref, r2_ref, t2_ref
):
    (u_c, v_c), (t_c, w_c) = corners(te_ref, to_ref, (U + 1) // 2), corners(te_ref, to_ref, (T + 1) // 2)
    (u_e, u_h), (v_e, v_h), (t_e, t_h), (w_e, w_h) = [halves(raw_ref, f) for f in (U, V, T, WET)]
    w_s, p_e, p_h = load(aux_ref, "w_s", "p_e", "p_h")
    p_c = [0.05 * s for s in level_sum(t_c, True)]

    (n_h, n_c), (b_h, b_c) = next_split(p_h, p_c), prev_split(p_h, p_c)
    u1_h = east_speed(u_h, v_h, n_h, b_h, w_h)
    u1_c = east_speed(u_c, v_c, n_c, b_c, w_c)
    (n_e, n_c), (b_e, b_c) = next_row(p_e, p_c), prev_row(p_e, p_c)
    v1_e = north_speed(u_e, v_e, n_e, b_e, w_e)
    v1_c = north_speed(u_c, v_c, n_c, b_c, w_c)
    heat_e, heat_h, cols_e, rows_h = load(aux_ref, "heat_e", "heat_h", "cols_e", "rows_h")
    rows_e = plus(next_row(t_e, t_c)[0], prev_row(t_e, t_c)[0])
    t1_e = warmed(t_e, heat_e, rows_e, cols_e, w_e)
    cols_h = plus(next_split(t_h, t_c)[0], prev_split(t_h, t_c)[0])
    t1_h = warmed(t_h, heat_h, rows_h, cols_h, w_h)
    fc_h, fc_c = split_factor(u1_h, u1_c, w_h, w_c)
    save(fc_ref, fc_h + fc_c)
    fr_e, fr_c = row_factor(v1_e, v1_c, w_e, w_c)
    save(fr_ref, fr_e + fr_c)

    u1_s, u1_e, v1_s, v1_h, t1_s, _, heat2 = load(
        aux_ref, "u1_s", "u1_e", "v1_s", "v1_h", "t1_s", "sun2", "heat2"
    )
    p1 = [0.05 * s for s in level_sum(t1_s + t1_e + t1_h, True)]
    p_s, p_e, p_h = p1[:2], p1[2:4], p1[4:]
    (n_s, n_e), (b_s, b_e) = next_split(p_s, p_e), prev_split(p_s, p_e)
    u2_s = east_speed(u1_s, v1_s, n_s, b_s, w_s)
    u2_e = east_speed(u1_e, v1_e, n_e, b_e, w_e)
    (n_s, n_h), (b_s, b_h) = next_row(p_s, p_h), prev_row(p_s, p_h)
    v2_s = north_speed(u1_s, v1_s, n_s, b_s, w_s)
    v2_h = north_speed(u1_h, v1_h, n_h, b_h, w_h)
    rows = plus(next_row(t1_s, t1_h)[0], prev_row(t1_s, t1_h)[0])
    cols = plus(next_split(t1_s, t1_e)[0], prev_split(t1_s, t1_e)[0])
    t2 = warmed(t1_s, heat2, rows, cols, w_s)

    save(t1_ref, t1_e + t1_h)
    save(t2_ref, t2)
    for k, x in enumerate((u2_s, v2_s, t2)):
        for i, tile in enumerate(plain(x)):
            for peer in range(ocean_ref.shape[0]):
                ocean_ref[peer, k, :, 128 * i : 128 * (i + 1)] = tile

    fc_s, fc_e = split_factor(u2_s, u2_e, w_s, w_e)
    save(c2_ref, fc_s + fc_e)
    fr_s, fr_h = row_factor(v2_s, v2_h, w_s, w_h)
    save(r2_ref, fr_s + fr_h)


def last_kernel(
    raw_ref, part_ref, aux_ref, te_ref, to_ref, stoich_ref, fc_ref, fr_ref, t1_ref, q1_ref,
    c2_ref, r2_ref, t2_ref, out_ref, q_ref, g_ref, g2_ref,
):
    def advect1(f, q_c):
        q_e, q_h = halves(raw_ref, f)
        fc, fr = load(fc_ref), load(fr_ref)
        row = row_divergence(q_e, q_c, fr[:2], fr[2:])[0]
        col = split_divergence(q_h, q_c, fc[:2], fc[2:])
        return minus(load(part_ref.at[f]), row + col)

    c = [corners(te_ref, to_ref, k) for k in range(3)]
    core_corners = [c[0][1], c[1][0], c[1][1], c[2][0], c[2][1]]
    first = [advect1(f, core_corners[f]) for f in range(5)]
    sun_e, sun_h = load(aux_ref, "sun_e", "sun_h")
    w_e, w_h = halves(raw_ref, WET)
    w_four, sun, t1_four, gain = w_e + w_h, sun_e + sun_h, load(t1_ref), []
    for i in range(4):
        core, g = reaction([first[f][i] for f in range(5)], sun[i], t1_four[i])
        gain.append(g)
        for f in range(5):
            q_ref[f, i] = (first[f][i] + 0.2 * core[f]) * w_four[i]
    save(g_ref, gain + w_four)

    def others1(k, _):
        both = corners(te_ref, to_ref, k)
        for j in range(2):
            f = 2 * k - 1 + j
            s = stoich_ref[f - 5]
            g = load(g_ref)
            out = each(lambda a, g, w: (a + s * g) * w, advect1(f, both[j]), g[:4], g[4:])
            save(q_ref.at[f], out)
        return 0

    lax.fori_loop(3, 10, others1, 0, unroll=7)

    w_s, sun2 = load(aux_ref, "w_s", "sun2")
    t2 = load(t2_ref)

    def advect2(f):
        q_s, x = load(q1_ref.at[f]), load(q_ref.at[f])
        fc, fr = load(c2_ref), load(r2_ref)
        row = row_divergence(q_s, x[2:], fr[:2], fr[2:])[0]
        return minus(minus(q_s, split_divergence(q_s, x[:2], fc[:2], fc[2:])), row)

    def finish(f, tiles):
        for i, x in enumerate(plain(tiles)):
            out_ref[f, 0, :, 128 * i : 128 * (i + 1)] = x

    first = [advect2(f) for f in range(5)]
    done = [[] for _ in range(5)]
    gain = []
    for i in range(2):
        core, g = reaction([first[f][i] for f in range(5)], sun2[i], t2[i])
        gain.append(g)
        for f in range(5):
            done[f].append((first[f][i] + 0.2 * core[f]) * w_s[i])
    for f in range(5):
        finish(f, done[f])
    save(g2_ref, gain + w_s)

    def others2(f, _):
        s = stoich_ref[f - 5]
        k = load(g2_ref)
        finish(f, each(lambda a, g, w: (a + s * g) * w, advect2(f), k[:2], k[2:]))
        return 0

    lax.fori_loop(5, NTR, others2, 0, unroll=7)


def swaps(count, first, place=lambda i: i):
    pairs = []
    for a in range(first, count - 1, 2):
        pairs += [(place(a), place(a + 1)), (place(a + 1), place(a))]
    return pairs


def far_pairs(bands, tiles):
    later, sooner = [], []
    for ty in range(bands):
        for a in range(1, tiles - 1, 2):
            pair = (ty * tiles + a, ty * tiles + a + 1)
            part = 4 * (a + 1) // tiles
            if part == 1 or (part == 2 and 4 * ty < 3 * bands):
                pair = pair[::-1]
            later.append(pair)
            sooner.append(pair[::-1])
    return later, sooner


def shards(ocean, tracers, bottom, stoich):
    comps = lax.axis_size("comp")
    bands = lax.axis_size("ty")
    tiles = lax.axis_size("tx")
    vmem = pl.BlockSpec(memory_space=VMEM)

    def arr(*dims):
        return VMEM(dims, jnp.float32)

    def near(*args):
        return [pltpu.with_memory_space_constraint(a, VMEM) for a in args]

    def place(row):
        return (row % comps) * bands + row // comps

    axes = ("comp", "ty")
    count = comps * bands

    def kernel(body, outs, ins, scratch=(), scalars=False):
        return pl.pallas_call(
            body,
            out_shape=tuple(outs),
            in_specs=[vmem] * ins + [pl.BlockSpec(memory_space=pltpu.SMEM)] * scalars,
            out_specs=(vmem,) * len(outs),
            scratch_shapes=[VMEM((*n, *TILE), jnp.float32) for n in scratch],
        )

    packed, first, rest, yields = kernel(
        pack_kernel,
        [arr(n, *TILE) for n in (2 * FIELDS + 1, PAIRS, PAIRS + FIELDS + 1, NTR - 5)],
        3,
        scalars=True,
    )(ocean, tracers, bottom.T, stoich)
    later, sooner = far_pairs(bands, tiles)

    grid = ("ty", "tx")
    first_a = lax.ppermute(first, grid, later)
    rest_a = lax.ppermute(rest, grid, later)
    first_b = lax.ppermute(first, grid, sooner)
    rest_b = lax.ppermute(rest, grid, sooner)
    chip = lax.ppermute(packed, "tx", swaps(tiles, 0))
    up, down, first = kernel(
        row_kernel, [arr(n, *TILE) for n in (WET + 1 + PAIRS, WET + 1 + PAIRS, PAIRS)], 4
    )(*near(packed, chip, first_a, first_b))
    is_odd = odd("comp")
    to = lax.ppermute(jnp.where(is_odd, down, up), axes, swaps(count, 1, place))
    te = lax.ppermute(jnp.where(is_odd, up, down), axes, swaps(count, 0, place))
    columns = kernel(
        cols_kernel,
        [arr(FIELDS + 1, 2, *TILE), arr(FIELDS + 1, 2, *TILE), arr(NTR, 4, *TILE), arr(12, *TILE)],
        5,
        [(FIELDS + 1,), (6,)],
    )(*near(packed, chip, first, rest_a, rest_b))
    state = kernel(
        own_kernel,
        [
            arr(FIELDS + 1, 4, *TILE),
            arr(NTR, 4, *TILE),
            arr(NTR, 2, *TILE),
            arr(2 * len(AUX), *TILE),
        ],
        7,
        [(4,), (4,)],
    )(*near(*columns, te, to, yields))
    raw, part, q1_own, aux = near(*state)
    rows, fc, fr, t1, c2, r2, t2 = kernel(
        ocean_kernel,
        [arr(comps, 3, ROWS, 256)] + [arr(n, *TILE) for n in (4, 4, 4, 4, 4, 2)],
        4,
    )(raw, aux, *near(te, to))
    gathered = lax.all_to_all(rows, "comp", 0, 0, tiled=True)
    (tracers_out,) = kernel(
        last_kernel,
        [jax.ShapeDtypeStruct((NTR, 1, ROWS, 256), jnp.float32)],
        13,
        [(NTR, 4), (8,), (4,)],
    )(raw, part, aux, *near(te, to, yields, fc, fr, t1), q1_own, *near(c2, r2, t2))
    return jnp.swapaxes(gathered, 0, 1).reshape(3, comps * ROWS, 256), tracers_out


def solution(mesh):
    in_specs = (P(None, "ty", "tx"), P(None, "ty", "comp", "tx"), P("ty", "tx"), P())
    out_specs = (P(None, "ty", "tx"), P(None, "ty", "comp", "tx"))
    return jax.shard_map(shards, mesh=mesh, in_specs=in_specs, out_specs=out_specs, check_vma=False)
```
